512 devices in a mesh: gx: 16 (over z_hi, x, core), gy: 32 (over y, z_lo).
Axes of the slice: x: 4, y: 8, z: 8 (z_hi: 2, z_lo: 4; z = z_hi * 4 + z_lo), core: 2. Of those that a mesh axis runs over, the one named last changes fastest.
Arguments:
- saturation: float32 [32, 32, 64, 4096], P('gx', 'gy'), may hold values from 0.05 to 0.95
- porosity: float32 [32, 32, 4096], P('gx', 'gy'), may hold values from 0.05 to 0.35
- observed_cells: int32 [32, 32, 512], P('gx', 'gy'), may hold values from 0 to 4095
- observed_values: float32 [32, 32, 512], P('gx', 'gy'), may hold values from -6 to 6
- error_variance: float32 [32, 32, 512], P('gx', 'gy'), may hold values from 0.1 to 1
- observed_count: int32 [32, 32], P('gx', 'gy'), may hold values from 64 to 512, as said below
- perturbation: bfloat16 [2, 32, 32, 64, 512], P(None, 'gx', 'gy'), may hold values from -5 to 5
- input_weight: float32 [2, 32], replicated, may hold values from -8 to 8
- input_bias: float32 [32], replicated, may hold values from -4 to 4
- output_weight: float32 [32], replicated, may hold values from -1 to 1
- output_bias: float32 [1], replicated, may hold values from -2 to 2
Outputs:
- saturation_out: float32 [32, 32, 64, 4096], P('gx', 'gy')
The draws below stay inside these ranges and needn't reach their ends.
Inputs may be any that keep to these rules, and one draw needn't show every extreme that they name: Tile t uses the observations in slots 0 to observed_count[t] - 1; some tile of the grid has exactly 512.
All inputs are finite; a program needn't handle non-finite values.
Results may differ from the reference program's by a relative error of at most 0.002.
Values may be sent and summed in bfloat16 or wider, within the bound.
A program may use at most 64 MiB of HBM per device.

```python
import math
import jax
import jax.numpy as jnp
from jax import lax

MEMBER_TOTAL = 64
TILE_SIDE = 64
MLP_WIDTH = 32
MAX_OBSERVED = 512
TAPER_REACH = 2
DATA_STEPS = 2
ALL_ROW_TILES = 32
ALL_COLUMN_TILES = 32
TILE_CELLS = 4096


def draw_observed_count(key, part):
    first_key, second_key, third_key = jax.random.split(key, 3)
    first_factor = jax.random.randint(first_key, (ALL_ROW_TILES, ALL_COLUMN_TILES), 0, 8)
    second_factor = jax.random.randint(second_key, (ALL_ROW_TILES, ALL_COLUMN_TILES), 0, 8)
    realization_tallies = MEMBER_TOTAL + first_factor * second_factor * (MAX_OBSERVED - MEMBER_TOTAL) // 49
    chosen = jax.random.randint(third_key, (), 0, ALL_ROW_TILES * ALL_COLUMN_TILES)
    places = jnp.arange(ALL_ROW_TILES * ALL_COLUMN_TILES, dtype=jnp.int32).reshape(ALL_ROW_TILES, ALL_COLUMN_TILES)
    return jnp.where(places == chosen, MAX_OBSERVED, realization_tallies).astype(jnp.int32)


def place_ends(entries, key, low, largest):
    longest = entries.shape.index(max(entries.shape))
    spots = []
    for shift in (0, 1):
        where = [jax.random.randint(jax.random.fold_in(key, axis), (), 0, length) for axis, length in enumerate(entries.shape)]
        where[longest] = (where[longest] + shift) % entries.shape[longest]
        spots.append(tuple(where))
    return entries.at[spots[0]].set(low).at[spots[1]].set(largest)


def shard_levels(key, extent, pieces, low, high):
    def one(axis_at, blocks):
        heights = jax.random.uniform(jax.random.fold_in(jax.random.fold_in(key, 6), axis_at), (blocks,), jnp.float32, low / len(pieces), high / len(pieces))
        return jnp.repeat(jnp.exp(heights), extent[axis_at] // blocks).reshape((-1,) + (1,) * (len(extent) - axis_at - 1))

    gain = one(*pieces[0])
    for cut in pieces[1:]:
        gain = gain * one(*cut)
    return gain


def bell_draw(own_key, shape, spread, limit, shards=(), kind=jnp.bfloat16):
    loudness = shard_levels(own_key, shape, shards, -0.22, 0.18) if shards else 1.0
    result = jax.random.normal(own_key, shape, jnp.float32) * spread * loudness
    return jnp.minimum(jnp.maximum(result, -limit), limit).astype(kind)


def setup_inputs(seed: int = 0) -> dict:
    key_of = jax.random.split(jax.random.key(seed), 12)
    return {
        "saturation": jnp.clip(0.05 + 0.9 * jax.random.uniform(key_of[0], (ALL_ROW_TILES, ALL_COLUMN_TILES, MEMBER_TOTAL, TILE_CELLS), jnp.float32) ** shard_levels(key_of[0], (ALL_ROW_TILES, ALL_COLUMN_TILES, MEMBER_TOTAL, TILE_CELLS), ((0, 16), (1, 32)), -0.2, 0.2), 0.05, 0.95),
        "porosity": jnp.clip(0.05 + 0.29999999 * jax.random.uniform(key_of[1], (ALL_ROW_TILES, ALL_COLUMN_TILES, TILE_CELLS), jnp.float32) ** shard_levels(key_of[1], (ALL_ROW_TILES, ALL_COLUMN_TILES, TILE_CELLS), ((0, 16), (1, 32)), -0.2, 0.2), 0.05, 0.35),
        "observed_cells": place_ends(jax.random.randint(key_of[2], (ALL_ROW_TILES, ALL_COLUMN_TILES, MAX_OBSERVED), 0, TILE_CELLS), jax.random.fold_in(key_of[2], 1), 0, TILE_CELLS - 1).astype(jnp.int32),
        "observed_values": bell_draw(key_of[3], (ALL_ROW_TILES, ALL_COLUMN_TILES, MAX_OBSERVED), 1.0, 6.0, ((0, 16), (1, 32)), jnp.float32),
        "error_variance": jnp.clip(jnp.exp(math.log(1.0) - 2.3025851 * jax.random.uniform(key_of[4], (ALL_ROW_TILES, ALL_COLUMN_TILES, MAX_OBSERVED), jnp.float32) ** shard_levels(key_of[4], (ALL_ROW_TILES, ALL_COLUMN_TILES, MAX_OBSERVED), ((0, 16), (1, 32)), -0.2, 0.2)), 0.1, 1.0),
        "observed_count": draw_observed_count(jax.random.fold_in(key_of[11], 71), 0),
        "perturbation": bell_draw(key_of[6], (DATA_STEPS, ALL_ROW_TILES, ALL_COLUMN_TILES, MEMBER_TOTAL, MAX_OBSERVED), 1.0, 5.0, ((1, 16), (2, 32))),
        "input_weight": bell_draw(key_of[7], (2, MLP_WIDTH), 2.0, 8.0, (), jnp.float32),
        "input_bias": bell_draw(key_of[8], (MLP_WIDTH,), 1.0, 4.0, (), jnp.float32),
        "output_weight": bell_draw(key_of[9], (MLP_WIDTH,), MLP_WIDTH ** -0.5, 1.0, (), jnp.float32),
        "output_bias": bell_draw(key_of[10], (1,), 0.5, 2.0, (), jnp.float32),
    }


def forward_model(entries_out, lithology_amounts, input_weight, input_bias, output_weight, output_bias):
    preactivation = input_weight[0][:, None, None] * entries_out[None] + (input_weight[1][:, None] * lithology_amounts[None, :] + input_bias[:, None])[:, None, :]
    return lax.optimization_barrier(jnp.sum(output_weight[:, None, None] * jnp.tanh(preactivation), axis=0)) + output_bias[0]

def patch_shares(fluid_fraction_samples, rockphysics_patch, chosen_indices, field_readings, shock_spread, random_shocks, realization_tallies, first_line_entries, widen_uncertainty, perceptron_weights):
    entries_out = jnp.take(fluid_fraction_samples, chosen_indices, axis=1)
    lithology_amounts = jnp.take(rockphysics_patch, chosen_indices)
    prior_predictions = forward_model(entries_out, lithology_amounts, perceptron_weights[0], perceptron_weights[1], perceptron_weights[2], perceptron_weights[3])
    departures_from_mean = prior_predictions - lax.optimization_barrier(jnp.mean(prior_predictions, axis=0, keepdims=True))
    mismatch_gaps = field_readings[None, :] + jnp.sqrt(widen_uncertainty * shock_spread)[None, :] * random_shocks.astype(jnp.float32) - prior_predictions
    active = (first_line_entries + jnp.arange(chosen_indices.shape[0], dtype=jnp.int32) < realization_tallies).astype(jnp.float32)
    scaled = departures_from_mean * (active / shock_spread)[None, :]
    spread_coupling = jnp.dot(scaled, departures_from_mean.T, precision=lax.Precision.HIGHEST)
    coupling_pieces = jnp.dot(scaled, mismatch_gaps.T, precision=lax.Precision.HIGHEST)
    return (spread_coupling, coupling_pieces)

def taper_sum(padded, row_tiles, column_tiles):
    tapered = jnp.zeros(padded[:row_tiles, :column_tiles].shape, padded.dtype)
    for shift_row in range(-TAPER_REACH, TAPER_REACH + 1):
        for shift_column in range(-TAPER_REACH, TAPER_REACH + 1):
            weight = math.exp(-(shift_row * shift_row + shift_column * shift_column) / (2.0 * TAPER_REACH * TAPER_REACH))
            tapered = tapered + weight * padded[TAPER_REACH + shift_row:TAPER_REACH + shift_row + row_tiles, TAPER_REACH + shift_column:TAPER_REACH + shift_column + column_tiles]
    return tapered

def blend_weights(tile_side):
    centred = (jnp.arange(tile_side, dtype=jnp.float32) + 0.5) / tile_side - 0.5
    offsets = jnp.arange(-1, 2, dtype=jnp.int32).astype(jnp.float32)
    hat_rows = jnp.maximum(0.0, 1.0 - jnp.abs(centred[None, :] - offsets[:, None]))
    return (hat_rows[:, None, :, None] * hat_rows[None, :, None, :]).reshape(9, tile_side * tile_side)

def renew_tile(fluid_fraction_samples, nearby, blend_table):
    realization_fields = fluid_fraction_samples.shape[0]
    departures_from_mean = fluid_fraction_samples - lax.optimization_barrier(jnp.mean(fluid_fraction_samples, axis=0, keepdims=True))
    weighted = (departures_from_mean[None] * blend_table[:, None, :]).astype(jnp.bfloat16).reshape(9 * realization_fields, -1)
    change = lax.dot_general(nearby.reshape(9 * realization_fields, realization_fields).astype(jnp.float32), weighted.astype(jnp.float32), (((0,), (0,)), ((), ())), preferred_element_type=jnp.float32)
    return fluid_fraction_samples + change

def reference(saturation, porosity, observed_cells, observed_values, error_variance, observed_count, perturbation, input_weight, input_bias, output_weight, output_bias):
    tile_count = ALL_ROW_TILES * ALL_COLUMN_TILES
    widen_always = jnp.full((DATA_STEPS,), float(DATA_STEPS), jnp.float32)
    blend_table = blend_weights(TILE_SIDE)
    perceptron_weights = (input_weight, input_bias, output_weight, output_bias)
    fluid_fraction_samples = saturation.reshape(tile_count, MEMBER_TOTAL, TILE_CELLS)
    lithology_amounts = porosity.reshape(tile_count, TILE_CELLS)
    chosen_indices = observed_cells.reshape(tile_count, MAX_OBSERVED)
    field_readings = observed_values.reshape(tile_count, MAX_OBSERVED)
    shock_spread = error_variance.reshape(tile_count, MAX_OBSERVED)
    realization_tallies = observed_count.reshape(tile_count)
    for piece_ordinal in range(DATA_STEPS):
        widen_uncertainty = widen_always[piece_ordinal]
        random_shocks = perturbation[piece_ordinal].reshape(tile_count, MEMBER_TOTAL, MAX_OBSERVED)

        def statistics(patch_pieces):
            return patch_shares(patch_pieces[0], patch_pieces[1], patch_pieces[2], patch_pieces[3], patch_pieces[4], patch_pieces[5], patch_pieces[6], 0, widen_uncertainty, perceptron_weights)
        spread_coupling, coupling_pieces = lax.map(statistics, (fluid_fraction_samples, lithology_amounts, chosen_indices, field_readings, shock_spread, random_shocks, realization_tallies))
        stacked = jnp.stack([spread_coupling, coupling_pieces], 1).reshape(ALL_ROW_TILES, ALL_COLUMN_TILES, 2, MEMBER_TOTAL * MEMBER_TOTAL)
        padded = jnp.pad(stacked, ((TAPER_REACH, TAPER_REACH), (TAPER_REACH, TAPER_REACH), (0, 0), (0, 0)))
        tapered_correction = taper_sum(padded, ALL_ROW_TILES, ALL_COLUMN_TILES).reshape(tile_count, 2, MEMBER_TOTAL, MEMBER_TOTAL)
        linear_operator = tapered_correction[:, 0] + (MEMBER_TOTAL - 1) * widen_uncertainty * jnp.eye(MEMBER_TOTAL, dtype=jnp.float32)[None]
        update_transform = jnp.linalg.solve(linear_operator, tapered_correction[:, 1])
        flat_transform = update_transform.astype(jnp.bfloat16).reshape(ALL_ROW_TILES, ALL_COLUMN_TILES, MEMBER_TOTAL * MEMBER_TOTAL)
        widened = jnp.pad(flat_transform, ((1, 1), (1, 1), (0, 0)), mode='edge')
        nearby = jnp.stack([widened[1 + shift_row:1 + shift_row + ALL_ROW_TILES, 1 + shift_column:1 + shift_column + ALL_COLUMN_TILES] for shift_row in (-1, 0, 1) for shift_column in (-1, 0, 1)], 2).reshape(tile_count, 9, MEMBER_TOTAL * MEMBER_TOTAL)

        def renew_pair(patch_pieces):
            return renew_tile(patch_pieces[0], patch_pieces[1], blend_table)
        fluid_fraction_samples = lax.map(renew_pair, (fluid_fraction_samples, nearby))
    return fluid_fraction_samples.reshape(ALL_ROW_TILES, ALL_COLUMN_TILES, MEMBER_TOTAL, TILE_CELLS)
```

```python
import functools
import math

import jax
import jax.numpy as jnp
from jax import lax
from jax.experimental import pallas as pl
from jax.experimental.pallas import tpu as pltpu
from jax.sharding import PartitionSpec as P

SIDE = 64
REACH = 2
STEPS = 2
LANES = 128
VMEM_LIMIT = 56 << 20
MESH = pl.DeviceIdType.MESH
HIGHEST = lax.Precision.HIGHEST
W1 = math.exp(-1.0 / (2.0 * REACH * REACH))
W2 = math.exp(-4.0 / (2.0 * REACH * REACH))


def network(s, p, w_ref, b_ref, v_ref, c_ref):
    total = jnp.zeros_like(s)
    for h in range(b_ref.shape[0]):
        inner = w_ref[0, h] * s + (w_ref[1, h] * p + b_ref[h])
        total = total + v_ref[h] * jnp.tanh(inner)
    return total + c_ref[0]


def products(predicted, observed, variance, count, shocks):
    slots = observed.shape[1]
    anomalies = predicted - jnp.mean(predicted, axis=0, keepdims=True)
    innovations = observed + jnp.sqrt(float(STEPS) * variance) * shocks - predicted
    active = lax.broadcasted_iota(jnp.int32, (1, slots), 1) < count
    scaled = anomalies * (jnp.where(active, 1.0, 0.0) / variance)
    both = jnp.concatenate([anomalies, innovations], axis=0)
    return lax.dot_general(
        scaled, both, (((1,), (1,)), ((), ())), precision=HIGHEST, preferred_element_type=jnp.float32
    )


def hat(x, offset):
    return jnp.maximum(0.0, 1.0 - jnp.abs(x - offset))


def centred(index):
    return (index.astype(jnp.float32) + 0.5) / SIDE - 0.5


def first_kernel(
    count_ref, w_ref, b_ref, v_ref, c_ref, sat_ref, por_ref, cell_ref, obs_ref, var_ref, pert_ref,
    gram_ref, sobs_ref, pobs_ref, pred_ref,
):
    tile = pl.program_id(0)
    members = sat_ref.shape[1]
    chunks = por_ref.shape[1]
    slots = cell_ref.shape[2]
    for block in range(slots // LANES):
        at = slice(block * LANES, (block + 1) * LANES)
        cells = cell_ref[0, :, at]
        low, high = cells & (LANES - 1), cells >> 7
        rows = lax.broadcasted_iota(jnp.int32, (chunks, LANES), 0)
        picked = jnp.take_along_axis(
            por_ref[0], jnp.broadcast_to(low, (chunks, LANES)), axis=1, mode="promise_in_bounds"
        )
        p = jnp.sum(jnp.where(rows == high, picked, 0.0), axis=0, keepdims=True)
        pobs_ref[0, :, at] = p
        low = jnp.broadcast_to(low, (members, LANES))
        high = jnp.broadcast_to(high, (members, LANES))
        s = jnp.zeros((members, LANES), jnp.float32)
        for chunk in range(chunks):
            part = sat_ref[0, :, chunk * LANES : (chunk + 1) * LANES]
            got = jnp.take_along_axis(part, low, axis=1, mode="promise_in_bounds")
            s = jnp.where(high == chunk, got, s)
        sobs_ref[0, :, at] = s
        pred_ref[:, at] = network(s, p, w_ref, b_ref, v_ref, c_ref)
    gram_ref[0] = products(
        pred_ref[...], obs_ref[0], var_ref[0], count_ref[tile], pert_ref[0, 0].astype(jnp.float32)
    )


def eliminate(matrices):
    members = matrices[0].shape[0]
    row_of = lax.broadcasted_iota(jnp.int32, matrices[0].shape, 0)
    for k in range(0, members, 2):
        done = []
        for m in matrices:
            r0, r1 = m[k : k + 1, :], m[k + 1 : k + 2, :]
            c0, c1 = m[:, k : k + 1], m[:, k + 1 : k + 2]
            a, b = m[k : k + 1, k : k + 1], m[k : k + 1, k + 1 : k + 2]
            c, d = m[k + 1 : k + 2, k : k + 1], m[k + 1 : k + 2, k + 1 : k + 2]
            inv = 1.0 / (a * d - b * c)
            t0 = (d * inv) * r0 - (b * inv) * r1
            t1 = (a * inv) * r1 - (c * inv) * r0
            m = m - (c0 * t0 + c1 * t1)
            m = jnp.where(row_of == k, t0, m)
            done.append(jnp.where(row_of == k + 1, t1, m))
        matrices = done
    return matrices


def second_kernel(
    count_ref, w_ref, b_ref, v_ref, c_ref, gram_ref, sobs_ref, pobs_ref, cell_ref, obs_ref, var_ref, pert_ref,
    blend_ref,
    own, up_down, summed, side, near, seen, pred, send_sem, recv_sem,
):
    nx, ny = lax.axis_size("gx"), lax.axis_size("gy")
    gx, gy = lax.axis_index("gx"), lax.axis_index("gy")
    tiles, members, slots = sobs_ref.shape

    up_down[...] = jnp.zeros_like(up_down)
    side[...] = jnp.zeros_like(side)
    near[...] = jnp.zeros_like(near)

    def exists(dx, dy):
        there = True
        if dx:
            there = jnp.logical_and(gx + dx >= 0, gx + dx < nx)
        if dy:
            along = jnp.logical_and(gy + dy >= 0, gy + dy < ny)
            there = along if there is True else jnp.logical_and(there, along)
        return there

    def device(dx, dy):
        return (jnp.clip(gx + dx, 0, nx - 1), jnp.clip(gy + dy, 0, ny - 1))

    rows = [(-1, 0), (1, 0)]
    columns = [(0, -2), (0, -1), (0, 1), (0, 2)]
    around = [(dx, dy) for dx in (-1, 0, 1) for dy in (-1, 0, 1) if dx or dy]

    barrier = pltpu.get_barrier_semaphore()
    partners = sorted(set(rows + columns + around))
    for dx, dy in partners:

        @pl.when(exists(dx, dy))
        def _(dx=dx, dy=dy):
            pl.semaphore_signal(barrier, inc=1, device_id=device(dx, dy), device_id_type=MESH)

    with jax.named_scope("meet"):
      pl.semaphore_wait(barrier, sum(jnp.where(exists(dx, dy), 1, 0) for dx, dy in partners))

    def copy(step, slot, src, dst, dx, dy):
        return pltpu.make_async_remote_copy(
            src_ref=src,
            dst_ref=dst,
            send_sem=send_sem.at[step, slot],
            recv_sem=recv_sem.at[step, slot],
            device_id=device(dx, dy),
            device_id_type=MESH,
        )

    def exchange(step, first, moves):
        copies = [
            (copy(step, first + i, src, dst, dx, dy), dx, dy) for i, (src, dst, dx, dy) in enumerate(moves)
        ]
        for one, dx, dy in copies:
            pl.when(exists(dx, dy))(one.start)
        for one, dx, dy in copies:
            pl.when(exists(-dx, -dy))(one.wait_recv)
        for one, dx, dy in copies:
            pl.when(exists(dx, dy))(one.wait_send)

    widen = (members - 1) * float(STEPS)
    eye = jnp.where(
        lax.broadcasted_iota(jnp.int32, (members, LANES), 0)
        == lax.broadcasted_iota(jnp.int32, (members, LANES), 1),
        widen,
        0.0,
    )
    seen[...] = sobs_ref[...]
    own[0] = gram_ref[...]
    for step in range(STEPS):
        with jax.named_scope("rows"):
          exchange(
            step, 0, [(own.at[step], up_down.at[step, i], dx, dy) for i, (dx, dy) in enumerate(rows)]
        )
        mine = own[step]
        below, above = up_down[step, 0], up_down[step, 1]
        summed[step, 0] = mine[0] + W1 * mine[1] + (W2 * above[0] + W1 * above[1]) + W2 * below[0]
        summed[step, 1] = mine[1] + W1 * mine[0] + W2 * above[1] + (W1 * below[0] + W2 * below[1])
        with jax.named_scope("columns"):
          exchange(
            step, 2, [(summed.at[step], side.at[step, i], dx, dy) for i, (dx, dy) in enumerate(columns)]
        )
        matrices = []
        for tile in range(tiles):
            matrices.append(
                eye
                + summed[step, tile]
                + W1 * (side[step, 1, tile] + side[step, 2, tile])
                + W2 * (side[step, 0, tile] + side[step, 3, tile])
            )
        with jax.named_scope("eliminate"):
            solved = eliminate(matrices)
        for tile in range(tiles):
            turned = jnp.transpose(solved[tile][:, members : 2 * members])
            half = members // 2
            near[step, 1, 1 + tile] = jnp.concatenate([turned[:half], turned[half:]], axis=1).astype(
                jnp.bfloat16
            )
        moves = []
        for dx, dy in around:
            if dx == 1:
                src, dst = near.at[step, 1, 2], near.at[step, 1 - dy, 0]
            elif dx == -1:
                src, dst = near.at[step, 1, 1], near.at[step, 1 - dy, 3]
            else:
                src, dst = near.at[step, 1, 1:3], near.at[step, 1 - dy, 1:3]
            moves.append((src, dst, dx, dy))
        with jax.named_scope("around"):
            exchange(step, 6, moves)

        @pl.when(gx == 0)
        def _():
            near[step, :, 0] = near[step, :, 1]

        @pl.when(gx == nx - 1)
        def _():
            near[step, :, 3] = near[step, :, 2]

        @pl.when(gy == 0)
        def _():
            near[step, 0] = near[step, 1]

        @pl.when(gy == ny - 1)
        def _():
            near[step, 2] = near[step, 1]

        for tile in range(tiles):
            pieces = []
            for a in range(3):
                packed = [near[step, b, tile + a] for b in range(3)]
                for start in (0, members):
                    pieces.append(
                        jnp.concatenate([one[:, start : start + members] for one in packed], axis=1)
                    )
            blend = jnp.concatenate(pieces, axis=0)
            blend_ref[step, tile] = blend
            if step + 1 == STEPS:
                continue
            s = seen[tile]
            cells = cell_ref[tile]
            x_row, x_column = centred(cells >> 6), centred(cells & (SIDE - 1))
            departures = s - jnp.mean(s, axis=0, keepdims=True)
            weighted = jnp.concatenate(
                [(departures * hat(x_column, b - 1.0)).astype(jnp.bfloat16) for b in range(3)], axis=0
            )
            moved = jnp.dot(blend, weighted, preferred_element_type=jnp.float32)
            for a in range(3):
                s = s + hat(x_row, a - 1.0) * moved[a * members : (a + 1) * members]
            seen[tile] = s
        if step + 1 == STEPS:
            continue
        for tile in range(tiles):
            for block in range(slots // LANES):
                at = slice(block * LANES, (block + 1) * LANES)
                pred[:, at] = network(seen[tile, :, at], pobs_ref[tile, :, at], w_ref, b_ref, v_ref, c_ref)
            own[step + 1, tile] = products(
                pred[...], obs_ref[tile], var_ref[tile], count_ref[tile], pert_ref[step + 1, tile].astype(jnp.float32)
            )


def third_kernel(blend_ref, sat_ref, out_ref):
    tile, block = pl.program_id(0), pl.program_id(1)
    members, width = sat_ref.shape[1:]
    half = block // (pl.num_programs(1) // 2)
    cells = lax.broadcasted_iota(jnp.int32, (1, width), 1) + block * width
    x_row, x_column = centred(cells >> 6), centred(cells & (SIDE - 1))
    offset = (half - 1).astype(jnp.float32)
    first_hat, second_hat = hat(x_row, offset), hat(x_row, offset + 1.0)
    s = sat_ref[0]
    for step in range(STEPS):
        departures = s - jnp.mean(s, axis=0, keepdims=True)
        weighted = jnp.concatenate(
            [(departures * hat(x_column, b - 1.0)).astype(jnp.bfloat16) for b in range(3)], axis=0
        )
        start = pl.multiple_of(half * members, members)
        blend = blend_ref[step, tile, pl.ds(start, 2 * members), :]
        moved = jnp.dot(blend, weighted, preferred_element_type=jnp.float32)
        s = s + (first_hat * moved[:members] + second_hat * moved[members:])
    out_ref[0] = s


def per_device(
    saturation, porosity, observed_cells, observed_values, error_variance, observed_count, perturbation,
    input_weight, input_bias, output_weight, output_bias,
):
    row_tiles, column_tiles, members, tile_cells = saturation.shape
    slots = observed_cells.shape[2]
    tiles = row_tiles * column_tiles
    sat = saturation.reshape(tiles, members, tile_cells)
    por = porosity.reshape(tiles, tile_cells // LANES, LANES)
    cells = observed_cells.reshape(tiles, 1, slots)
    values = observed_values.reshape(tiles, 1, slots)
    variance = error_variance.reshape(tiles, 1, slots)
    count = observed_count.reshape(tiles)
    pert = perturbation.reshape(STEPS, tiles, members, slots)

    smem = pl.BlockSpec(memory_space=pltpu.SMEM)
    vmem = pl.BlockSpec(memory_space=pltpu.VMEM)

    def per_tile(*shape):
        return pl.BlockSpec((1,) + shape, lambda t: (t,) + (0,) * len(shape))

    weights = (input_weight, input_bias, output_weight, output_bias)
    gram, sobs, pobs = pl.pallas_call(
        first_kernel,
        name="observe",
        grid=(tiles,),
        out_shape=[
            jax.ShapeDtypeStruct((tiles, members, 2 * members), jnp.float32),
            jax.ShapeDtypeStruct((tiles, members, slots), jnp.float32),
            jax.ShapeDtypeStruct((tiles, 1, slots), jnp.float32),
        ],
        in_specs=[smem] * 5
        + [
            per_tile(members, tile_cells),
            per_tile(tile_cells // LANES, LANES),
            per_tile(1, slots),
            per_tile(1, slots),
            per_tile(1, slots),
            pl.BlockSpec((1, 1, members, slots), lambda t: (0, t, 0, 0)),
        ],
        out_specs=[per_tile(members, 2 * members), per_tile(members, slots), per_tile(1, slots)],
        scratch_shapes=[pltpu.VMEM((members, slots), jnp.float32)],
        compiler_params=pltpu.CompilerParams(vmem_limit_bytes=VMEM_LIMIT),
    )(count, *weights, sat, por, cells, values, variance, pert)

    blend = pl.pallas_call(
        second_kernel,
        name="exchange",
        out_shape=jax.ShapeDtypeStruct((STEPS, tiles, 3 * members, 3 * members), jnp.bfloat16),
        in_specs=[smem] * 5 + [vmem] * 7,
        out_specs=vmem,
        scratch_shapes=[
            pltpu.VMEM((STEPS, tiles, members, LANES), jnp.float32),
            pltpu.VMEM((STEPS, 2, tiles, members, LANES), jnp.float32),
            pltpu.VMEM((STEPS, tiles, members, LANES), jnp.float32),
            pltpu.VMEM((STEPS, 4, tiles, members, LANES), jnp.float32),
            pltpu.VMEM((STEPS, 3, tiles + 2, members // 2, LANES), jnp.bfloat16),
            pltpu.VMEM((tiles, members, slots), jnp.float32),
            pltpu.VMEM((members, slots), jnp.float32),
            pltpu.SemaphoreType.DMA((STEPS, 14)),
            pltpu.SemaphoreType.DMA((STEPS, 14)),
        ],
        compiler_params=pltpu.CompilerParams(
            collective_id=0, has_side_effects=True, vmem_limit_bytes=VMEM_LIMIT
        ),
    )(count, *weights, gram, sobs, pobs, cells, values, variance, pert)

    blocks = 4
    width = tile_cells // blocks
    posterior = pl.pallas_call(
        third_kernel,
        name="update",
        grid=(tiles, blocks),
        out_shape=jax.ShapeDtypeStruct(sat.shape, sat.dtype),
        in_specs=[vmem, pl.BlockSpec((1, members, width), lambda t, b: (t, 0, b))],
        out_specs=pl.BlockSpec((1, members, width), lambda t, b: (t, 0, b)),
        compiler_params=pltpu.CompilerParams(vmem_limit_bytes=VMEM_LIMIT),
    )(blend, sat)
    return posterior.reshape(row_tiles, column_tiles, members, tile_cells)


def solution(mesh):
    tile = P("gx", "gy", None)
    return jax.shard_map(
        per_device,
        mesh=mesh,
        in_specs=(
            P("gx", "gy", None, None), tile, tile, tile, tile, P("gx", "gy"),
            P(None, "gx", "gy", None, None), P(), P(), P(), P(),
        ),
        out_specs=P("gx", "gy", None, None),
        check_vma=False,
    )
```

```python
import math

import jax
import jax.numpy as jnp
from jax import lax
from jax.experimental import pallas as pl
from jax.experimental.pallas import tpu as pltpu
from jax.sharding import PartitionSpec as P

SIDE = 64
REACH = 2
STEPS = 2
LANES = 128
VMEM_LIMIT = 56 << 20
MESH = pl.DeviceIdType.MESH
HIGHEST = lax.Precision.HIGHEST
W1 = math.exp(-1.0 / (2.0 * REACH * REACH))
W2 = math.exp(-4.0 / (2.0 * REACH * REACH))


def network(s, p, w_ref, b_ref, v_ref, c_ref):
    total = jnp.zeros_like(s)
    for h in range(b_ref.shape[0]):
        inner = w_ref[0, h] * s + (w_ref[1, h] * p + b_ref[h])
        total = total + v_ref[h] * jnp.tanh(inner)
    return total + c_ref[0]


def products(predicted, observed, variance, count, shocks):
    slots = observed.shape[1]
    anomalies = predicted - jnp.mean(predicted, axis=0, keepdims=True)
    innovations = observed + jnp.sqrt(float(STEPS) * variance) * shocks - predicted
    active = lax.broadcasted_iota(jnp.int32, (1, slots), 1) < count
    scaled = anomalies * (jnp.where(active, 1.0, 0.0) / variance)
    both = jnp.concatenate([anomalies, innovations], axis=0)
    return lax.dot_general(
        scaled, both, (((1,), (1,)), ((), ())), precision=HIGHEST, preferred_element_type=jnp.float32
    )


def hat(x, offset):
    return jnp.maximum(0.0, 1.0 - jnp.abs(x - offset))


def centred(index):
    return (index.astype(jnp.float32) + 0.5) / SIDE - 0.5


def eliminate(matrices):
    group, width = 8, matrices[0].shape[1]
    groups = matrices[0].shape[0] // group
    row = lax.broadcasted_iota(jnp.int32, (group, width), 0)
    parts = [[m[group * h : group * (h + 1)] for h in range(groups)] for m in matrices]
    for g in range(groups):
        done = []
        for m in parts:
            pivots = [
                jnp.broadcast_to(m[g][:, group * g + i : group * g + i + 1], (group, width))
                for i in range(group)
            ]
            fresh = m[g]
            for j in range(group):
                inverse = 1.0 / pivots[j][j : j + 1]
                factor = jnp.where(row == j, -1.0, pivots[j])
                fresh = jnp.where(row == j, 0.0, fresh) - factor * (fresh[j : j + 1] * inverse)
                for i in range(j + 1, group):
                    pivots[i] = jnp.where(row == j, 0.0, pivots[i]) - factor * (pivots[i][j : j + 1] * inverse)
            new = []
            for h in range(groups):
                if h == g:
                    new.append(fresh)
                    continue
                taken = m[h][:, group * g : group * g + 1] * fresh[0:1]
                for i in range(1, group):
                    taken = taken + m[h][:, group * g + i : group * g + i + 1] * fresh[i : i + 1]
                new.append(m[h] - taken)
            done.append(new)
        parts = done
    return [jnp.concatenate(m, axis=0) for m in parts]


def whole_kernel(
    count_ref, w_ref, b_ref, v_ref, c_ref,
    sat_hbm, por_hbm, cell_hbm, obs_hbm, var_hbm, pert_hbm,
    out_hbm,
    sat, por, cell, obs, var, pert, load_sem, store_sem,
    own, up_down, summed, side, near, seen, where_p, pred, ready, ready_seen, blend,
    send_sem, recv_sem,
):
    nx, ny = lax.axis_size("gx"), lax.axis_size("gy")
    gx, gy = lax.axis_index("gx"), lax.axis_index("gy")
    tiles, members, tile_cells = sat.shape
    slots = seen.shape[2]
    chunks = tile_cells // LANES

    small = [(por_hbm, por), (cell_hbm, cell), (obs_hbm, obs), (var_hbm, var), (pert_hbm, pert)]
    loads = [pltpu.make_async_copy(src, dst, load_sem.at[i]) for i, (src, dst) in enumerate(small)]
    loads += [
        pltpu.make_async_copy(sat_hbm.at[t], sat.at[t], load_sem.at[len(small) + t]) for t in range(tiles)
    ]
    for load in loads:
        load.start()

    up_down[...] = jnp.zeros_like(up_down)
    side[...] = jnp.zeros_like(side)
    near[...] = jnp.zeros_like(near)

    def exists(dx, dy):
        there = True
        if dx:
            there = jnp.logical_and(gx + dx >= 0, gx + dx < nx)
        if dy:
            along = jnp.logical_and(gy + dy >= 0, gy + dy < ny)
            there = along if there is True else jnp.logical_and(there, along)
        return there

    def device(dx, dy):
        return (jnp.clip(gx + dx, 0, nx - 1), jnp.clip(gy + dy, 0, ny - 1))

    rows = [(-1, 0), (1, 0)]
    columns = [(0, -2), (0, 2), (0, -1), (0, 1)]
    around = [(dx, dy) for dx in (-1, 1, 0) for dy in (-1, 1, 0) if dx or dy]

    barrier = pltpu.get_barrier_semaphore()
    partners = sorted(set(rows + columns + around))
    for dx, dy in partners:

        @pl.when(exists(dx, dy))
        def _(dx=dx, dy=dy):
            pl.semaphore_signal(barrier, inc=1, device_id=device(dx, dy), device_id_type=MESH)

    late = []

    def start(step, first, moves):
        copies = []
        for i, (src, dst, dx, dy) in enumerate(moves):
            one = pltpu.make_async_remote_copy(
                src_ref=src,
                dst_ref=dst,
                send_sem=send_sem.at[step, first + i],
                recv_sem=recv_sem.at[step, first + i],
                device_id=device(dx, dy),
                device_id_type=MESH,
            )
            pl.when(exists(dx, dy))(one.start)
            copies.append((one, dx, dy))
        late.extend(copies)
        return copies

    def receive(copies):
        for one, dx, dy in copies:
            pl.when(exists(-dx, -dy))(one.wait_recv)

    def gather(tile, at):
        cells = cell[tile, :, at]
        low, high = cells & (LANES - 1), cells >> 7
        line = lax.broadcasted_iota(jnp.int32, (chunks, LANES), 0)
        picked = jnp.take_along_axis(
            por[tile], jnp.broadcast_to(low, (chunks, LANES)), axis=1, mode="promise_in_bounds"
        )
        where_p[tile, :, at] = jnp.sum(jnp.where(line == high, picked, 0.0), axis=0, keepdims=True)
        low = jnp.broadcast_to(low, (members, LANES))
        high = jnp.broadcast_to(high, (members, LANES))
        s = jnp.zeros((members, LANES), jnp.float32)
        for chunk in range(chunks):
            part = sat[tile, :, chunk * LANES : (chunk + 1) * LANES]
            got = jnp.take_along_axis(part, low, axis=1, mode="promise_in_bounds")
            s = jnp.where(high == chunk, got, s)
        seen[tile, :, at] = s

    def statistics(step):
        def observe(block, carry):
            at = pl.ds(pl.multiple_of(block * LANES, LANES), LANES)
            for tile in range(tiles):
                pred[tile, :, at] = network(
                    seen[tile, :, at], where_p[tile, :, at], w_ref, b_ref, v_ref, c_ref
                )
            return carry

        lax.fori_loop(0, slots // LANES, observe, 0)
        for tile in range(tiles):
            own[step, tile] = products(
                pred[tile], obs[tile], var[tile], count_ref[tile], pert[step, tile].astype(jnp.float32)
            )

    def weigh(s, cells, offset, count):
        departures = s - jnp.mean(s, axis=0, keepdims=True)
        x_row, x_column = centred(cells >> 6), centred(cells & (SIDE - 1))
        return [
            (departures * (hat(x_row, offset + a) * hat(x_column, b - 1.0))).astype(jnp.bfloat16)
            for a in range(count)
            for b in range(3)
        ]

    part = 512
    per_half = tile_cells // 2 // part

    def prepare():
        for tile in range(tiles):
            for half in range(2):

                def body(i, carry):
                    first = pl.multiple_of(half * (tile_cells // 2) + i * part, part)
                    cells = lax.broadcasted_iota(jnp.int32, (1, part), 1) + first
                    pieces = weigh(sat[tile, :, pl.ds(first, part)], cells, half - 1.0, 2)
                    for q, piece in enumerate(pieces):
                        ready[tile, q * members : (q + 1) * members, pl.ds(first, part)] = piece
                    return carry

                lax.fori_loop(0, per_half, body, 0)

    def apply(tile):
        for half in range(2):
            matrix = blend[tile, :, 3 * members * half : 3 * members * (half + 2)]

            def body(i, carry):
                first = pl.multiple_of(half * (tile_cells // 2) + i * part, part)
                at = pl.ds(first, part)
                moved = jnp.dot(matrix, ready[tile, :, at], preferred_element_type=jnp.float32)
                sat[tile, :, at] = sat[tile, :, at] + moved
                return carry

            lax.fori_loop(0, per_half, body, 0)

    for load in loads:
        load.wait()
    for tile in range(tiles):

        def body(block, carry, tile=tile):
            gather(tile, pl.ds(pl.multiple_of(block * LANES, LANES), LANES))
            return carry

        lax.fori_loop(0, slots // LANES, body, 0)
    statistics(0)

    widen = (members - 1) * float(STEPS)
    eye = jnp.where(
        lax.broadcasted_iota(jnp.int32, (members, LANES), 0)
        == lax.broadcasted_iota(jnp.int32, (members, LANES), 1),
        widen,
        0.0,
    )
    pl.semaphore_wait(barrier, sum(jnp.where(exists(dx, dy), 1, 0) for dx, dy in partners))

    for step in range(STEPS):
        last = step + 1 == STEPS
        copies = start(
            step, 0, [(own.at[step], up_down.at[step, i], dx, dy) for i, (dx, dy) in enumerate(rows)]
        )
        if last:
            for tile in range(tiles):
                apply(tile)
        else:
            for tile in range(tiles):
                pieces = weigh(seen[tile], cell[tile], -1.0, 3)
                for q, piece in enumerate(pieces):
                    ready_seen[tile, q * members : (q + 1) * members] = piece
        receive(copies)
        mine = own[step]
        below, above = up_down[step, 0], up_down[step, 1]
        summed[step, 0] = mine[0] + W1 * mine[1] + (W2 * above[0] + W1 * above[1]) + W2 * below[0]
        summed[step, 1] = mine[1] + W1 * mine[0] + W2 * above[1] + (W1 * below[0] + W2 * below[1])
        copies = start(
            step, 2, [(summed.at[step], side.at[step, i], dx, dy) for i, (dx, dy) in enumerate(columns)]
        )
        prepare()
        receive(copies)
        matrices = []
        for tile in range(tiles):
            matrices.append(
                eye
                + summed[step, tile]
                + W1 * (side[step, 2, tile] + side[step, 3, tile])
                + W2 * (side[step, 0, tile] + side[step, 1, tile])
            )
        solved = eliminate(matrices)
        half = members // 2
        for tile in range(tiles):
            turned = jnp.transpose(solved[tile][:, members : 2 * members])
            near[step, 1, 1 + tile] = jnp.concatenate([turned[:half], turned[half:]], axis=1).astype(
                jnp.bfloat16
            )
        moves = []
        for dx, dy in around:
            if dx == 1:
                src, dst = near.at[step, 1, 2], near.at[step, 1 - dy, 0]
            elif dx == -1:
                src, dst = near.at[step, 1, 1], near.at[step, 1 - dy, 3]
            else:
                src, dst = near.at[step, 1, 1:3], near.at[step, 1 - dy, 1:3]
            moves.append((src, dst, dx, dy))
        receive(start(step, 6, moves))

        @pl.when(gx == 0)
        def _():
            near[step, :, 0] = near[step, :, 1]

        @pl.when(gx == nx - 1)
        def _():
            near[step, :, 3] = near[step, :, 2]

        @pl.when(gy == 0)
        def _():
            near[step, 0] = near[step, 1]

        @pl.when(gy == ny - 1)
        def _():
            near[step, 2] = near[step, 1]

        for tile in range(tiles):
            packed = [near[step, b, tile + a] for a in range(3) for b in range(3)]
            for q in range(2):
                blend[tile, q * half : (q + 1) * half] = jnp.concatenate(
                    [one[:, q * members : (q + 1) * members] for one in packed], axis=1
                )
            if not last:
                moved = jnp.dot(blend[tile], ready_seen[tile], preferred_element_type=jnp.float32)
                seen[tile] = seen[tile] + moved
        if not last:
            statistics(step + 1)

    stores = []
    for tile in range(tiles):
        apply(tile)
        store = pltpu.make_async_copy(sat.at[tile], out_hbm.at[tile], store_sem.at[tile])
        store.start()
        stores.append(store)
    for one, dx, dy in late:
        pl.when(exists(dx, dy))(one.wait_send)
    for store in stores:
        store.wait()


def per_device(
    saturation, porosity, observed_cells, observed_values, error_variance, observed_count, perturbation,
    input_weight, input_bias, output_weight, output_bias,
):
    row_tiles, column_tiles, members, tile_cells = saturation.shape
    slots = observed_cells.shape[2]
    tiles = row_tiles * column_tiles
    arrays = (
        saturation.reshape(tiles, members, tile_cells),
        porosity.reshape(tiles, tile_cells // LANES, LANES),
        observed_cells.reshape(tiles, 1, slots),
        observed_values.reshape(tiles, 1, slots),
        error_variance.reshape(tiles, 1, slots),
        perturbation.reshape(STEPS, tiles, members, slots),
    )
    scalars = (observed_count.reshape(tiles), input_weight, input_bias, output_weight, output_bias)
    f32, bf16 = jnp.float32, jnp.bfloat16
    posterior = pl.pallas_call(
        whole_kernel,
        name="assimilate",
        out_shape=jax.ShapeDtypeStruct((tiles, members, tile_cells), f32),
        in_specs=[pl.BlockSpec(memory_space=pltpu.SMEM)] * len(scalars)
        + [pl.BlockSpec(memory_space=pl.ANY)] * len(arrays),
        out_specs=pl.BlockSpec(memory_space=pl.ANY),
        scratch_shapes=[pltpu.VMEM(a.shape, a.dtype) for a in arrays]
        + [
            pltpu.SemaphoreType.DMA((len(arrays) - 1 + tiles,)),
            pltpu.SemaphoreType.DMA((tiles,)),
            pltpu.VMEM((STEPS, tiles, members, LANES), f32),
            pltpu.VMEM((STEPS, 2, tiles, members, LANES), f32),
            pltpu.VMEM((STEPS, tiles, members, LANES), f32),
            pltpu.VMEM((STEPS, 4, tiles, members, LANES), f32),
            pltpu.VMEM((STEPS, 3, tiles + 2, members // 2, LANES), bf16),
            pltpu.VMEM((tiles, members, slots), f32),
            pltpu.VMEM((tiles, 1, slots), f32),
            pltpu.VMEM((tiles, members, slots), f32),
            pltpu.VMEM((tiles, 6 * members, tile_cells), bf16),
            pltpu.VMEM((tiles, 9 * members, slots), bf16),
            pltpu.VMEM((tiles, members, 9 * members), bf16),
            pltpu.SemaphoreType.DMA((STEPS, 14)),
            pltpu.SemaphoreType.DMA((STEPS, 14)),
        ],
        compiler_params=pltpu.CompilerParams(
            collective_id=0, has_side_effects=True, vmem_limit_bytes=VMEM_LIMIT
        ),
    )(*scalars, *arrays)
    return posterior.reshape(row_tiles, column_tiles, members, tile_cells)


def solution(mesh):
    tile = P("gx", "gy", None)
    return jax.shard_map(
        per_device,
        mesh=mesh,
        in_specs=(
            P("gx", "gy", None, None), tile, tile, tile, tile, P("gx", "gy"),
            P(None, "gx", "gy", None, None), P(), P(), P(), P(),
        ),
        out_specs=P("gx", "gy", None, None),
        check_vma=False,
    )
```

```python
import math

import jax
import jax.numpy as jnp
from jax import lax
from jax.experimental import pallas as pl
from jax.experimental.pallas import tpu as pltpu
from jax.sharding import PartitionSpec as P

SIDE = 64
REACH = 2
STEPS = 2
LANES = 128
VMEM_LIMIT = 24 << 20
MESH = pl.DeviceIdType.MESH
HIGHEST = lax.Precision.HIGHEST
W1 = math.exp(-1.0 / (2.0 * REACH * REACH))
W2 = math.exp(-4.0 / (2.0 * REACH * REACH))


def network(s, p, w_ref, b_ref, v_ref, c_ref):
    total = jnp.zeros_like(s)
    for h in range(b_ref.shape[0]):
        inner = w_ref[0, h] * s + (w_ref[1, h] * p + b_ref[h])
        total = total + v_ref[h] * jnp.tanh(inner)
    return total + c_ref[0]


def products(predicted, observed, variance, count, shocks):
    slots = observed.shape[1]
    anomalies = predicted - jnp.mean(predicted, axis=0, keepdims=True)
    innovations = observed + jnp.sqrt(float(STEPS) * variance) * shocks - predicted
    active = lax.broadcasted_iota(jnp.int32, (1, slots), 1) < count
    scaled = anomalies * (jnp.where(active, 1.0, 0.0) / variance)
    both = jnp.concatenate([anomalies, innovations], axis=0)
    return lax.dot_general(
        scaled, both, (((1,), (1,)), ((), ())), precision=HIGHEST, preferred_element_type=jnp.float32
    )


def hat(x, offset):
    return jnp.maximum(0.0, 1.0 - jnp.abs(x - offset))


def centred(index):
    return (index.astype(jnp.float32) + 0.5) / SIDE - 0.5


def eliminate(matrices):
    group, width = 8, matrices[0].shape[1]
    groups = matrices[0].shape[0] // group
    row = lax.broadcasted_iota(jnp.int32, (group, width), 0)
    parts = [[m[group * h : group * (h + 1)] for h in range(groups)] for m in matrices]
    for g in range(groups):
        done = []
        for m in parts:
            pivots = [
                jnp.broadcast_to(m[g][:, group * g + i : group * g + i + 1], (group, width))
                for i in range(group)
            ]
            fresh = m[g]
            for j in range(group):
                inverse = 1.0 / pivots[j][j : j + 1]
                factor = jnp.where(row == j, -1.0, pivots[j])
                fresh = jnp.where(row == j, 0.0, fresh) - factor * (fresh[j : j + 1] * inverse)
                for i in range(j + 1, group):
                    pivots[i] = jnp.where(row == j, 0.0, pivots[i]) - factor * (pivots[i][j : j + 1] * inverse)
            new = []
            for h in range(groups):
                if h == g:
                    new.append(fresh)
                    continue
                taken = m[h][:, group * g : group * g + 1] * fresh[0:1]
                for i in range(1, group):
                    taken = taken + m[h][:, group * g + i : group * g + i + 1] * fresh[i : i + 1]
                new.append(m[h] - taken)
            done.append(new)
        parts = done
    return [jnp.concatenate(m, axis=0) for m in parts]


def whole_kernel(
    count_hbm, w_hbm, b_hbm, v_hbm, c_hbm,
    sat_hbm, por_hbm, cell_hbm, obs_hbm, var_hbm, pert_hbm,
    out_ref,
    count_ref, w_ref, b_ref, v_ref, c_ref,
    sat, por, cell, obs, var, pert, load_sem,
    own, up_down, summed, side, near, seen, where_p, pred, ready, ready_seen, blend,
    send_sem, recv_sem,
):
    nx, ny = lax.axis_size("gx"), lax.axis_size("gy")
    gx, gy = lax.axis_index("gx"), lax.axis_index("gy")
    tiles, members, tile_cells = sat.shape
    slots = seen.shape[2]
    chunks = tile_cells // LANES

    small = [(count_hbm, count_ref), (w_hbm, w_ref), (b_hbm, b_ref), (v_hbm, v_ref), (c_hbm, c_ref)]
    small += [(por_hbm, por), (cell_hbm, cell), (obs_hbm, obs), (var_hbm, var), (pert_hbm, pert)]
    loads = [pltpu.make_async_copy(src, dst, load_sem.at[i]) for i, (src, dst) in enumerate(small)]
    loads += [
        pltpu.make_async_copy(sat_hbm.at[t], sat.at[t], load_sem.at[len(small) + t]) for t in range(tiles)
    ]
    for load in loads:
        load.start()

    up_down[...] = jnp.zeros_like(up_down)
    side[...] = jnp.zeros_like(side)
    near[...] = jnp.zeros_like(near)

    def exists(dx, dy):
        there = True
        if dx:
            there = jnp.logical_and(gx + dx >= 0, gx + dx < nx)
        if dy:
            along = jnp.logical_and(gy + dy >= 0, gy + dy < ny)
            there = along if there is True else jnp.logical_and(there, along)
        return there

    def device(dx, dy):
        return (jnp.clip(gx + dx, 0, nx - 1), jnp.clip(gy + dy, 0, ny - 1))

    rows = [(-1, 0), (1, 0)]
    columns = [(0, -2), (0, 2), (0, -1), (0, 1)]
    around = [(dx, dy) for dx in (-1, 1, 0) for dy in (-1, 1, 0) if dx or dy]

    barrier = pltpu.get_barrier_semaphore()
    partners = sorted(set(rows + columns + around))
    for dx, dy in partners:

        @pl.when(exists(dx, dy))
        def _(dx=dx, dy=dy):
            pl.semaphore_signal(barrier, inc=1, device_id=device(dx, dy), device_id_type=MESH)

    late = []

    def start(step, first, moves):
        copies = []
        for i, (src, dst, dx, dy) in enumerate(moves):
            one = pltpu.make_async_remote_copy(
                src_ref=src,
                dst_ref=dst,
                send_sem=send_sem.at[step, first + i],
                recv_sem=recv_sem.at[step, first + i],
                device_id=device(dx, dy),
                device_id_type=MESH,
            )
            pl.when(exists(dx, dy))(one.start)
            copies.append((one, dx, dy))
        late.extend(copies)
        return copies

    def receive(copies):
        for one, dx, dy in copies:
            pl.when(exists(-dx, -dy))(one.wait_recv)

    def gather(tile, at):
        cells = cell[tile, :, at]
        low, high = cells & (LANES - 1), cells >> 7
        line = lax.broadcasted_iota(jnp.int32, (chunks, LANES), 0)
        picked = jnp.take_along_axis(
            por[tile], jnp.broadcast_to(low, (chunks, LANES)), axis=1, mode="promise_in_bounds"
        )
        where_p[tile, :, at] = jnp.sum(jnp.where(line == high, picked, 0.0), axis=0, keepdims=True)
        low = jnp.broadcast_to(low, (members, LANES))
        high = jnp.broadcast_to(high, (members, LANES))
        s = jnp.zeros((members, LANES), jnp.float32)
        for chunk in range(chunks):
            part = sat[tile, :, chunk * LANES : (chunk + 1) * LANES]
            got = jnp.take_along_axis(part, low, axis=1, mode="promise_in_bounds")
            s = jnp.where(high == chunk, got, s)
        seen[tile, :, at] = s

    def statistics(step):
        def observe(block, carry):
            at = pl.ds(pl.multiple_of(block * LANES, LANES), LANES)
            for tile in range(tiles):
                pred[tile, :, at] = network(
                    seen[tile, :, at], where_p[tile, :, at], w_ref, b_ref, v_ref, c_ref
                )
            return carry

        lax.fori_loop(0, slots // LANES, observe, 0)
        for tile in range(tiles):
            own[step, tile] = products(
                pred[tile], obs[tile], var[tile], count_ref[tile], pert[step, tile].astype(jnp.float32)
            )

    def weigh(s, cells, offset, count):
        departures = s - jnp.mean(s, axis=0, keepdims=True)
        x_row, x_column = centred(cells >> 6), centred(cells & (SIDE - 1))
        return [
            (departures * (hat(x_row, offset + a) * hat(x_column, b - 1.0))).astype(jnp.bfloat16)
            for a in range(count)
            for b in range(3)
        ]

    part = tile_cells // 2

    def place(half):
        cells = lax.broadcasted_iota(jnp.int32, (1, part), 1) + half * part
        return centred(cells >> 6), centred(cells & (SIDE - 1))

    def prepare(tile):
        for half in range(2):
            x_row, x_column = place(half)
            at = slice(half * part, (half + 1) * part)
            s = sat[tile, :, at]
            departures = s - jnp.mean(s, axis=0, keepdims=True)
            beside = jnp.where(x_column < 0.0, hat(x_column, -1.0), hat(x_column, 1.0))
            for q in range(4):
                factor = hat(x_row, half - 1.0 + q // 2) * (beside if q % 2 else hat(x_column, 0.0))
                ready[tile, q * members : (q + 1) * members, at] = (departures * factor).astype(jnp.bfloat16)

    def arrange(step, tile):
        for half in range(2):
            for b in range(2):
                for q in range(2):
                    row = b * members + q * (members // 2)
                    blend[tile, half, row : row + members // 2] = jnp.concatenate(
                        [
                            near[step, (1, 2 * b)[beside], tile + half + a][:, q * members : (q + 1) * members]
                            for a in range(2)
                            for beside in range(2)
                        ],
                        axis=1,
                    )

    def apply(tile, into):
        for half in range(2):
            at = slice(half * part, (half + 1) * part)
            moved = jnp.dot(blend[tile, half], ready[tile, :, at], preferred_element_type=jnp.float32)
            left = jnp.broadcast_to(place(half)[1] < 0.0, (members, part))
            into[tile, :, at] = sat[tile, :, at] + jnp.where(left, moved[:members], moved[members:])

    for load in loads:
        load.wait()
    for tile in range(tiles):

        def body(block, carry, tile=tile):
            gather(tile, pl.ds(pl.multiple_of(block * LANES, LANES), LANES))
            return carry

        lax.fori_loop(0, slots // LANES, body, 0)
    statistics(0)

    widen = (members - 1) * float(STEPS)
    eye = jnp.where(
        lax.broadcasted_iota(jnp.int32, (members, LANES), 0)
        == lax.broadcasted_iota(jnp.int32, (members, LANES), 1),
        widen,
        0.0,
    )
    pl.semaphore_wait(barrier, sum(jnp.where(exists(dx, dy), 1, 0) for dx, dy in partners))

    for step in range(STEPS):
        last = step + 1 == STEPS
        copies = start(
            step, 0, [(own.at[step], up_down.at[step, i], dx, dy) for i, (dx, dy) in enumerate(rows)]
        )
        if last:
            for tile in range(tiles):
                arrange(step - 1, tile)
                apply(tile, sat)
        else:
            for tile in range(tiles):
                pieces = weigh(seen[tile], cell[tile], -1.0, 3)
                for q, piece in enumerate(pieces):
                    ready_seen[tile, q * members : (q + 1) * members] = piece
        receive(copies)
        mine = own[step]
        below, above = up_down[step, 0], up_down[step, 1]
        summed[step, 0] = mine[0] + W1 * mine[1] + (W2 * above[0] + W1 * above[1]) + W2 * below[0]
        summed[step, 1] = mine[1] + W1 * mine[0] + W2 * above[1] + (W1 * below[0] + W2 * below[1])
        copies = start(
            step, 2, [(summed.at[step], side.at[step, i], dx, dy) for i, (dx, dy) in enumerate(columns)]
        )
        for tile in range(tiles):
            prepare(tile)
        receive(copies)
        matrices = []
        for tile in range(tiles):
            matrices.append(
                eye
                + summed[step, tile]
                + W1 * (side[step, 2, tile] + side[step, 3, tile])
                + W2 * (side[step, 0, tile] + side[step, 1, tile])
            )
        solved = eliminate(matrices)
        half = members // 2
        for tile in range(tiles):
            turned = jnp.transpose(solved[tile][:, members : 2 * members])
            near[step, 1, 1 + tile] = jnp.concatenate([turned[:half], turned[half:]], axis=1).astype(
                jnp.bfloat16
            )
        moves = []
        for dx, dy in around:
            if dx == 1:
                src, dst = near.at[step, 1, 2], near.at[step, 1 - dy, 0]
            elif dx == -1:
                src, dst = near.at[step, 1, 1], near.at[step, 1 - dy, 3]
            else:
                src, dst = near.at[step, 1, 1:3], near.at[step, 1 - dy, 1:3]
            moves.append((src, dst, dx, dy))
        receive(start(step, 6, moves))

        @pl.when(gx == 0)
        def _():
            near[step, :, 0] = near[step, :, 1]

        @pl.when(gx == nx - 1)
        def _():
            near[step, :, 3] = near[step, :, 2]

        @pl.when(gy == 0)
        def _():
            near[step, 0] = near[step, 1]

        @pl.when(gy == ny - 1)
        def _():
            near[step, 2] = near[step, 1]

        if not last:
            for tile in range(tiles):
                packed = [near[step, b, tile + a] for a in range(3) for b in range(3)]
                matrix = jnp.concatenate(
                    [
                        jnp.concatenate([one[:, q * members : (q + 1) * members] for one in packed], axis=1)
                        for q in range(2)
                    ],
                    axis=0,
                )
                moved = jnp.dot(matrix, ready_seen[tile], preferred_element_type=jnp.float32)
                seen[tile] = seen[tile] + moved
        if not last:
            statistics(step + 1)

    for tile in range(tiles):
        arrange(STEPS - 1, tile)
        apply(tile, out_ref)
    for one, dx, dy in late:
        pl.when(exists(dx, dy))(one.wait_send)


def per_device(
    saturation, porosity, observed_cells, observed_values, error_variance, observed_count, perturbation,
    input_weight, input_bias, output_weight, output_bias,
):
    row_tiles, column_tiles, members, tile_cells = saturation.shape
    slots = observed_cells.shape[2]
    tiles = row_tiles * column_tiles
    arrays = (
        saturation.reshape(tiles, members, tile_cells),
        porosity.reshape(tiles, tile_cells // LANES, LANES),
        observed_cells.reshape(tiles, 1, slots),
        observed_values.reshape(tiles, 1, slots),
        error_variance.reshape(tiles, 1, slots),
        perturbation.reshape(STEPS, tiles, members, slots),
    )
    scalars = (observed_count.reshape(tiles), input_weight, input_bias, output_weight, output_bias)
    f32, bf16 = jnp.float32, jnp.bfloat16
    posterior = pl.pallas_call(
        whole_kernel,
        name="assimilate",
        out_shape=jax.ShapeDtypeStruct((tiles, members, tile_cells), f32),
        in_specs=[pl.BlockSpec(memory_space=pltpu.HBM)] * (len(scalars) + len(arrays)),
        out_specs=pl.BlockSpec(memory_space=pltpu.VMEM),
        scratch_shapes=[pltpu.SMEM(a.shape, a.dtype) for a in scalars]
        + [pltpu.VMEM(a.shape, a.dtype) for a in arrays]
        + [
            pltpu.SemaphoreType.DMA((len(scalars) + len(arrays) - 1 + tiles,)),
            pltpu.VMEM((STEPS, tiles, members, LANES), f32),
            pltpu.VMEM((STEPS, 2, tiles, members, LANES), f32),
            pltpu.VMEM((STEPS, tiles, members, LANES), f32),
            pltpu.VMEM((STEPS, 4, tiles, members, LANES), f32),
            pltpu.VMEM((STEPS, 3, tiles + 2, members // 2, LANES), bf16),
            pltpu.VMEM((tiles, members, slots), f32),
            pltpu.VMEM((tiles, 1, slots), f32),
            pltpu.VMEM((tiles, members, slots), f32),
            pltpu.VMEM((tiles, 4 * members, tile_cells), bf16),
            pltpu.VMEM((tiles, 9 * members, slots), bf16),
            pltpu.VMEM((tiles, 2, 2 * members, 4 * members), bf16),
            pltpu.SemaphoreType.DMA((STEPS, 14)),
            pltpu.SemaphoreType.DMA((STEPS, 14)),
        ],
        compiler_params=pltpu.CompilerParams(
            collective_id=0, has_side_effects=True, vmem_limit_bytes=VMEM_LIMIT
        ),
    )(*(one if one.size == 1 else pltpu.with_memory_space_constraint(one, pltpu.HBM) for one in scalars + arrays))
    return posterior.reshape(row_tiles, column_tiles, members, tile_cells)


def solution(mesh):
    tile = P("gx", "gy", None)
    return jax.shard_map(
        per_device,
        mesh=mesh,
        in_specs=(
            P("gx", "gy", None, None), tile, tile, tile, tile, P("gx", "gy"),
            P(None, "gx", "gy", None, None), P(), P(), P(), P(),
        ),
        out_specs=P("gx", "gy", None, None),
        check_vma=False,
    )
```

```python
import math

import jax
import jax.numpy as jnp
from jax import lax
from jax.experimental import pallas as pl
from jax.experimental.pallas import tpu as pltpu
from jax.sharding import PartitionSpec as P

SIDE = 64
REACH = 2
STEPS = 2
LANES = 128
VMEM_LIMIT = 24 << 20
MESH = pl.DeviceIdType.MESH
HIGHEST = lax.Precision.HIGHEST
W1 = math.exp(-1.0 / (2.0 * REACH * REACH))
W2 = math.exp(-4.0 / (2.0 * REACH * REACH))


def network(s, p, w_ref, b_ref, v_ref, c_ref):
    total = jnp.zeros_like(s)
    for h in range(b_ref.shape[0]):
        inner = w_ref[0, h] * s + (w_ref[1, h] * p + b_ref[h])
        total = total + v_ref[h] * jnp.tanh(inner)
    return total + c_ref[0]


def products(predicted, observed, variance, count, shocks):
    slots = observed.shape[1]
    anomalies = predicted - jnp.mean(predicted, axis=0, keepdims=True)
    innovations = observed + jnp.sqrt(float(STEPS) * variance) * shocks - predicted
    active = lax.broadcasted_iota(jnp.int32, (1, slots), 1) < count
    scaled = anomalies * (jnp.where(active, 1.0, 0.0) / variance)
    both = jnp.concatenate([anomalies, innovations], axis=0)
    return lax.dot_general(
        both, scaled, (((1,), (1,)), ((), ())), precision=HIGHEST, preferred_element_type=jnp.float32
    )


def hat(x, offset):
    return jnp.maximum(0.0, 1.0 - jnp.abs(x - offset))


def centred(index):
    return (index.astype(jnp.float32) + 0.5) / SIDE - 0.5


def eliminate(matrices):
    group, width = 8, matrices[0].shape[1]
    groups = matrices[0].shape[0] // group
    row = lax.broadcasted_iota(jnp.int32, (group, width), 0)
    parts = [[m[group * h : group * (h + 1)] for h in range(groups)] for m in matrices]
    for g in range(groups):
        done = []
        for m in parts:
            pivots = [
                jnp.broadcast_to(m[g][:, group * g + i : group * g + i + 1], (group, width))
                for i in range(group)
            ]
            fresh = m[g]
            for j in range(group):
                inverse = 1.0 / pivots[j][j : j + 1]
                factor = jnp.where(row == j, -1.0, pivots[j])
                fresh = jnp.where(row == j, 0.0, fresh) - factor * (fresh[j : j + 1] * inverse)
                for i in range(j + 1, group):
                    pivots[i] = jnp.where(row == j, 0.0, pivots[i]) - factor * (pivots[i][j : j + 1] * inverse)
            new = []
            for h in range(groups):
                if h == g:
                    new.append(fresh)
                    continue
                taken = m[h][:, group * g : group * g + 1] * fresh[0:1]
                for i in range(1, group):
                    taken = taken + m[h][:, group * g + i : group * g + i + 1] * fresh[i : i + 1]
                new.append(m[h] - taken)
            done.append(new)
        parts = done
    return [jnp.concatenate(m, axis=0) for m in parts]


def whole_kernel(
    count_hbm, w_hbm, b_hbm, v_hbm, c_hbm,
    sat_hbm, por_hbm, cell_hbm, obs_hbm, var_hbm, pert_hbm,
    out_ref,
    count_ref, w_ref, b_ref, v_ref, c_ref,
    sat, por, cell, obs, var, pert, load_sem,
    own, up_down, summed, side, near, seen, where_p, pred, ready, ready_seen, blend,
    send_sem, recv_sem,
):
    nx, ny = lax.axis_size("gx"), lax.axis_size("gy")
    gx, gy = lax.axis_index("gx"), lax.axis_index("gy")
    tiles, members, tile_cells = sat.shape
    slots = seen.shape[2]
    chunks = tile_cells // LANES

    small = [(count_hbm, count_ref), (w_hbm, w_ref), (b_hbm, b_ref), (v_hbm, v_ref), (c_hbm, c_ref)]
    small += [(por_hbm, por), (cell_hbm, cell), (obs_hbm, obs), (var_hbm, var), (pert_hbm, pert)]
    loads = [pltpu.make_async_copy(src, dst, load_sem.at[i]) for i, (src, dst) in enumerate(small)]
    loads += [
        pltpu.make_async_copy(sat_hbm.at[t], sat.at[t], load_sem.at[len(small) + t]) for t in range(tiles)
    ]
    for load in loads:
        load.start()

    up_down[...] = jnp.zeros_like(up_down)
    side[...] = jnp.zeros_like(side)
    near[...] = jnp.zeros_like(near)

    def exists(dx, dy):
        there = True
        if dx:
            there = jnp.logical_and(gx + dx >= 0, gx + dx < nx)
        if dy:
            along = jnp.logical_and(gy + dy >= 0, gy + dy < ny)
            there = along if there is True else jnp.logical_and(there, along)
        return there

    def device(dx, dy):
        return (jnp.clip(gx + dx, 0, nx - 1), jnp.clip(gy + dy, 0, ny - 1))

    rows = [(-1, 0), (1, 0)]
    columns = [(0, -2), (0, 2), (0, -1), (0, 1)]
    around = [(dx, dy) for dx in (-1, 1, 0) for dy in (-1, 1, 0) if dx or dy]

    barrier = pltpu.get_barrier_semaphore()
    partners = sorted(set(rows + columns + around))
    for dx, dy in partners:

        @pl.when(exists(dx, dy))
        def _(dx=dx, dy=dy):
            pl.semaphore_signal(barrier, inc=1, device_id=device(dx, dy), device_id_type=MESH)

    late = []

    def start(step, first, moves):
        copies = []
        for i, (src, dst, dx, dy) in enumerate(moves):
            one = pltpu.make_async_remote_copy(
                src_ref=src,
                dst_ref=dst,
                send_sem=send_sem.at[step, first + i],
                recv_sem=recv_sem.at[step, first + i],
                device_id=device(dx, dy),
                device_id_type=MESH,
            )
            pl.when(exists(dx, dy))(one.start)
            copies.append((one, dx, dy))
        late.extend(copies)
        return copies

    def receive(copies):
        for one, dx, dy in copies:
            pl.when(exists(-dx, -dy))(one.wait_recv)

    def gather(tile, at):
        cells = cell[tile, :, at]
        low, high = cells & (LANES - 1), cells >> 7
        line = lax.broadcasted_iota(jnp.int32, (chunks, LANES), 0)
        picked = jnp.take_along_axis(
            por[tile], jnp.broadcast_to(low, (chunks, LANES)), axis=1, mode="promise_in_bounds"
        )
        where_p[tile, :, at] = jnp.sum(jnp.where(line == high, picked, 0.0), axis=0, keepdims=True)
        low = jnp.broadcast_to(low, (members, LANES))
        high = jnp.broadcast_to(high, (members, LANES))
        s = jnp.zeros((members, LANES), jnp.float32)
        for chunk in range(chunks):
            part = sat[tile, :, chunk * LANES : (chunk + 1) * LANES]
            got = jnp.take_along_axis(part, low, axis=1, mode="promise_in_bounds")
            s = jnp.where(high == chunk, got, s)
        seen[tile, :, at] = s

    def statistics(step):
        def observe(block, carry):
            at = pl.ds(pl.multiple_of(block * LANES, LANES), LANES)
            for tile in range(tiles):
                pred[tile, :, at] = network(
                    seen[tile, :, at], where_p[tile, :, at], w_ref, b_ref, v_ref, c_ref
                )
            return carry

        lax.fori_loop(0, slots // LANES, observe, 0)
        found = [
            products(pred[tile], obs[tile], var[tile], count_ref[tile], pert[step, tile].astype(jnp.float32))
            for tile in range(tiles)
        ]
        for kind in range(2):
            own[step, kind] = jnp.concatenate(
                [one[kind * members : (kind + 1) * members] for one in found], axis=1
            )

    def weigh(s, cells, offset, count):
        departures = s - jnp.mean(s, axis=0, keepdims=True)
        x_row, x_column = centred(cells >> 6), centred(cells & (SIDE - 1))
        return [
            (departures * (hat(x_row, offset + a) * hat(x_column, b - 1.0))).astype(jnp.bfloat16)
            for a in range(count)
            for b in range(3)
        ]

    part = tile_cells // 2

    def place(half):
        cells = lax.broadcasted_iota(jnp.int32, (1, part), 1) + half * part
        return centred(cells >> 6), centred(cells & (SIDE - 1))

    def prepare(tile):
        for half in range(2):
            x_row, x_column = place(half)
            at = slice(half * part, (half + 1) * part)
            s = sat[tile, :, at]
            departures = s - jnp.mean(s, axis=0, keepdims=True)
            beside = jnp.where(x_column < 0.0, hat(x_column, -1.0), hat(x_column, 1.0))
            for q in range(4):
                factor = hat(x_row, half - 1.0 + q // 2) * (beside if q % 2 else hat(x_column, 0.0))
                ready[tile, q * members : (q + 1) * members, at] = (departures * factor).astype(jnp.bfloat16)

    def arrange(step, tile):
        for half in range(2):
            for b in range(2):
                for q in range(2):
                    row = b * members + q * (members // 2)
                    blend[tile, half, row : row + members // 2] = jnp.concatenate(
                        [
                            near[step, (1, 2 * b)[beside], tile + half + a][:, q * members : (q + 1) * members]
                            for a in range(2)
                            for beside in range(2)
                        ],
                        axis=1,
                    )

    def apply(tile, into):
        for half in range(2):
            at = slice(half * part, (half + 1) * part)
            moved = jnp.dot(blend[tile, half], ready[tile, :, at], preferred_element_type=jnp.float32)
            left = jnp.broadcast_to(place(half)[1] < 0.0, (members, part))
            into[tile, :, at] = sat[tile, :, at] + jnp.where(left, moved[:members], moved[members:])

    for load in loads[:-tiles]:
        load.wait()
    for tile in range(tiles):
        loads[tile - tiles].wait()

        def body(block, carry, tile=tile):
            gather(tile, pl.ds(pl.multiple_of(block * LANES, LANES), LANES))
            return carry

        lax.fori_loop(0, slots // LANES, body, 0)
    statistics(0)

    widen = (members - 1) * float(STEPS)
    row_of = lax.broadcasted_iota(jnp.int32, (members, LANES), 0)
    lane_of = lax.broadcasted_iota(jnp.int32, (members, LANES), 1)
    first = lane_of < members
    unit = jnp.where(lane_of == row_of + members, 1.0, 0.0)
    diagonal = jnp.where((lane_of == row_of) | (lane_of == row_of + members), widen, 0.0)

    def swap(x):
        return jnp.concatenate([x[:, members:], x[:, :members]], axis=1)

    def sum_rows(step, kind):
        mine, below, above = own[step, kind], up_down[step, kind, 0], up_down[step, kind, 1]
        beside = W1 * (swap(mine) + jnp.where(first, swap(above), swap(below)))
        return mine + W2 * (above + below) + beside

    def sum_columns(step, kind):
        near_by, far = side[step, kind, 2] + side[step, kind, 3], side[step, kind, 0] + side[step, kind, 1]
        return summed[step, kind] + W1 * near_by + W2 * far

    pl.semaphore_wait(barrier, sum(jnp.where(exists(dx, dy), 1, 0) for dx, dy in partners))

    for step in range(STEPS):
        last = step + 1 == STEPS
        by_row = [
            start(
                step,
                2 * kind,
                [(own.at[step, kind], up_down.at[step, kind, i], dx, dy) for i, (dx, dy) in enumerate(rows)],
            )
            for kind in range(2)
        ]
        if last:
            for tile in range(tiles):
                arrange(step - 1, tile)
                apply(tile, sat)
        else:
            for tile in range(tiles):
                pieces = weigh(seen[tile], cell[tile], -1.0, 3)
                for q, piece in enumerate(pieces):
                    ready_seen[tile, q * members : (q + 1) * members] = piece
        by_column = []
        for kind in range(2):
            receive(by_row[kind])
            summed[step, kind] = sum_rows(step, kind)
            by_column.append(
                start(
                    step,
                    4 + 4 * kind,
                    [
                        (summed.at[step, kind], side.at[step, kind, i], dx, dy)
                        for i, (dx, dy) in enumerate(columns)
                    ],
                )
            )
        for tile in range(tiles):
            prepare(tile)
        receive(by_column[0])
        pair = sum_columns(step, 0) + diagonal
        inverses = eliminate([jnp.where(first, one, unit) for one in (pair, swap(pair))])
        receive(by_column[1])
        pair = sum_columns(step, 1)
        half = members // 2
        for tile in range(tiles):
            turned = jnp.dot(
                pair[:, tile * members : (tile + 1) * members],
                inverses[tile][:, members:],
                precision=HIGHEST,
                preferred_element_type=jnp.float32,
            )
            near[step, 1, 1 + tile] = jnp.concatenate([turned[:half], turned[half:]], axis=1).astype(
                jnp.bfloat16
            )
        moves = []
        for dx, dy in around:
            if dx == 1:
                src, dst = near.at[step, 1, 2], near.at[step, 1 - dy, 0]
            elif dx == -1:
                src, dst = near.at[step, 1, 1], near.at[step, 1 - dy, 3]
            else:
                src, dst = near.at[step, 1, 1:3], near.at[step, 1 - dy, 1:3]
            moves.append((src, dst, dx, dy))
        receive(start(step, 12, moves))

        @pl.when(gx == 0)
        def _():
            near[step, :, 0] = near[step, :, 1]

        @pl.when(gx == nx - 1)
        def _():
            near[step, :, 3] = near[step, :, 2]

        @pl.when(gy == 0)
        def _():
            near[step, 0] = near[step, 1]

        @pl.when(gy == ny - 1)
        def _():
            near[step, 2] = near[step, 1]

        if not last:
            for tile in range(tiles):
                packed = [near[step, b, tile + a] for a in range(3) for b in range(3)]
                matrix = jnp.concatenate(
                    [
                        jnp.concatenate([one[:, q * members : (q + 1) * members] for one in packed], axis=1)
                        for q in range(2)
                    ],
                    axis=0,
                )
                moved = jnp.dot(matrix, ready_seen[tile], preferred_element_type=jnp.float32)
                seen[tile] = seen[tile] + moved
        if not last:
            statistics(step + 1)

    for tile in range(tiles):
        arrange(STEPS - 1, tile)
        apply(tile, out_ref)
    for one, dx, dy in late:
        pl.when(exists(dx, dy))(one.wait_send)


def per_device(
    saturation, porosity, observed_cells, observed_values, error_variance, observed_count, perturbation,
    input_weight, input_bias, output_weight, output_bias,
):
    row_tiles, column_tiles, members, tile_cells = saturation.shape
    slots = observed_cells.shape[2]
    tiles = row_tiles * column_tiles
    arrays = (
        saturation.reshape(tiles, members, tile_cells),
        porosity.reshape(tiles, tile_cells // LANES, LANES),
        observed_cells.reshape(tiles, 1, slots),
        observed_values.reshape(tiles, 1, slots),
        error_variance.reshape(tiles, 1, slots),
        perturbation.reshape(STEPS, tiles, members, slots),
    )
    scalars = (observed_count.reshape(tiles), input_weight, input_bias, output_weight, output_bias)
    f32, bf16 = jnp.float32, jnp.bfloat16
    posterior = pl.pallas_call(
        whole_kernel,
        name="assimilate",
        out_shape=jax.ShapeDtypeStruct((tiles, members, tile_cells), f32),
        in_specs=[pl.BlockSpec(memory_space=pltpu.HBM)] * (len(scalars) + len(arrays)),
        out_specs=pl.BlockSpec(memory_space=pltpu.VMEM),
        scratch_shapes=[pltpu.SMEM(a.shape, a.dtype) for a in scalars]
        + [pltpu.VMEM(a.shape, a.dtype) for a in arrays]
        + [
            pltpu.SemaphoreType.DMA((len(scalars) + len(arrays) - 1 + tiles,)),
            pltpu.VMEM((STEPS, tiles, members, LANES), f32),
            pltpu.VMEM((STEPS, 2, 2, members, LANES), f32),
            pltpu.VMEM((STEPS, tiles, members, LANES), f32),
            pltpu.VMEM((STEPS, 2, 4, members, LANES), f32),
            pltpu.VMEM((STEPS, 3, tiles + 2, members // 2, LANES), bf16),
            pltpu.VMEM((tiles, members, slots), f32),
            pltpu.VMEM((tiles, 1, slots), f32),
            pltpu.VMEM((tiles, members, slots), f32),
            pltpu.VMEM((tiles, 4 * members, tile_cells), bf16),
            pltpu.VMEM((tiles, 9 * members, slots), bf16),
            pltpu.VMEM((tiles, 2, 2 * members, 4 * members), bf16),
            pltpu.SemaphoreType.DMA((STEPS, 20)),
            pltpu.SemaphoreType.DMA((STEPS, 20)),
        ],
        compiler_params=pltpu.CompilerParams(
            collective_id=0, has_side_effects=True, vmem_limit_bytes=VMEM_LIMIT
        ),
    )(*(one if one.size == 1 else pltpu.with_memory_space_constraint(one, pltpu.HBM) for one in scalars + arrays))
    return posterior.reshape(row_tiles, column_tiles, members, tile_cells)


def solution(mesh):
    tile = P("gx", "gy", None)
    return jax.shard_map(
        per_device,
        mesh=mesh,
        in_specs=(
            P("gx", "gy", None, None), tile, tile, tile, tile, P("gx", "gy"),
            P(None, "gx", "gy", None, None), P(), P(), P(), P(),
        ),
        out_specs=P("gx", "gy", None, None),
        check_vma=False,
    )
```

```python
import math

import jax
import jax.numpy as jnp
from jax import lax
from jax.experimental import pallas as pl
from jax.experimental.pallas import tpu as pltpu
from jax.sharding import PartitionSpec as P

SIDE = 64
REACH = 2
STEPS = 2
LANES = 128
VMEM_LIMIT = 24 << 20
MESH = pl.DeviceIdType.MESH
HIGHEST = lax.Precision.HIGHEST
W1 = math.exp(-1.0 / (2.0 * REACH * REACH))
W2 = math.exp(-4.0 / (2.0 * REACH * REACH))


def network(s, p, w_ref, b_ref, v_ref, c_ref):
    total = jnp.zeros_like(s)
    for h in range(b_ref.shape[0]):
        inner = w_ref[0, h] * s + (w_ref[1, h] * p + b_ref[h])
        total = total + v_ref[h] * jnp.tanh(inner)
    return total + c_ref[0]


def products(predicted, observed, variance, count, shocks):
    slots = observed.shape[1]
    anomalies = predicted - jnp.mean(predicted, axis=0, keepdims=True)
    innovations = observed + jnp.sqrt(float(STEPS) * variance) * shocks - predicted
    active = lax.broadcasted_iota(jnp.int32, (1, slots), 1) < count
    scaled = anomalies * (jnp.where(active, 1.0, 0.0) / variance)
    both = jnp.concatenate([anomalies, innovations], axis=0)
    return lax.dot_general(
        both, scaled, (((1,), (1,)), ((), ())), precision=HIGHEST, preferred_element_type=jnp.float32
    )


def hat(x, offset):
    return jnp.maximum(0.0, 1.0 - jnp.abs(x - offset))


def centred(index):
    return (index.astype(jnp.float32) + 0.5) / SIDE - 0.5


def eliminate(matrices):
    group, width = 8, matrices[0].shape[1]
    groups = matrices[0].shape[0] // group
    row = lax.broadcasted_iota(jnp.int32, (group, width), 0)
    parts = [[m[group * h : group * (h + 1)] for h in range(groups)] for m in matrices]
    for g in range(groups):
        done = []
        for m in parts:
            pivots = [
                jnp.broadcast_to(m[g][:, group * g + i : group * g + i + 1], (group, width))
                for i in range(group)
            ]
            fresh = m[g]
            for j in range(group):
                inverse = 1.0 / pivots[j][j : j + 1]
                factor = jnp.where(row == j, -1.0, pivots[j])
                fresh = jnp.where(row == j, 0.0, fresh) - factor * (fresh[j : j + 1] * inverse)
                for i in range(j + 1, group):
                    pivots[i] = jnp.where(row == j, 0.0, pivots[i]) - factor * (pivots[i][j : j + 1] * inverse)
            new = []
            for h in range(groups):
                if h == g:
                    new.append(fresh)
                    continue
                taken = m[h][:, group * g : group * g + 1] * fresh[0:1]
                for i in range(1, group):
                    taken = taken + m[h][:, group * g + i : group * g + i + 1] * fresh[i : i + 1]
                new.append(m[h] - taken)
            done.append(new)
        parts = done
    return [jnp.concatenate(m, axis=0) for m in parts]


def whole_kernel(
    count_hbm, w_hbm, b_hbm, v_hbm, c_hbm,
    sat_hbm, por_hbm, cell_hbm, obs_hbm, var_hbm, pert_hbm,
    out_ref,
    count_ref, w_ref, b_ref, v_ref, c_ref,
    sat, por, cell, obs, var, pert, load_sem,
    own, up_down, summed, side, near, seen, where_p, pred, ready, ready_seen, blend,
    send_sem, recv_sem,
):
    nx, ny = lax.axis_size("gx"), lax.axis_size("gy")
    gx, gy = lax.axis_index("gx"), lax.axis_index("gy")
    tiles, members, tile_cells = sat.shape
    slots = seen.shape[2]
    chunks = tile_cells // LANES

    small = [(count_hbm, count_ref), (w_hbm, w_ref), (b_hbm, b_ref), (v_hbm, v_ref), (c_hbm, c_ref)]
    small += [(por_hbm, por), (cell_hbm, cell), (obs_hbm, obs), (var_hbm, var), (pert_hbm, pert)]
    loads = [pltpu.make_async_copy(src, dst, load_sem.at[i]) for i, (src, dst) in enumerate(small)]
    loads += [
        pltpu.make_async_copy(sat_hbm.at[t], sat.at[t], load_sem.at[len(small) + t]) for t in range(tiles)
    ]
    for load in loads:
        load.start()

    up_down[...] = jnp.zeros_like(up_down)
    side[...] = jnp.zeros_like(side)
    near[...] = jnp.zeros_like(near)

    def exists(dx, dy):
        there = True
        if dx:
            there = jnp.logical_and(gx + dx >= 0, gx + dx < nx)
        if dy:
            along = jnp.logical_and(gy + dy >= 0, gy + dy < ny)
            there = along if there is True else jnp.logical_and(there, along)
        return there

    def device(dx, dy):
        return (jnp.clip(gx + dx, 0, nx - 1), jnp.clip(gy + dy, 0, ny - 1))

    rows = [(-1, 0), (1, 0)]
    columns = [(0, -2), (0, 2), (0, -1), (0, 1)]
    around = [(dx, dy) for dx in (-1, 1, 0) for dy in (-1, 1, 0) if dx or dy]

    barrier = pltpu.get_barrier_semaphore()
    partners = sorted(set(rows + columns + around))
    for dx, dy in partners:

        @pl.when(exists(dx, dy))
        def _(dx=dx, dy=dy):
            pl.semaphore_signal(barrier, inc=1, device_id=device(dx, dy), device_id_type=MESH)

    late = []

    def start(step, first, moves):
        copies = []
        for i, (src, dst, dx, dy) in enumerate(moves):
            one = pltpu.make_async_remote_copy(
                src_ref=src,
                dst_ref=dst,
                send_sem=send_sem.at[step, first + i],
                recv_sem=recv_sem.at[step, first + i],
                device_id=device(dx, dy),
                device_id_type=MESH,
            )
            pl.when(exists(dx, dy))(one.start)
            copies.append((one, dx, dy))
        late.extend(copies)
        return copies

    def receive(copies):
        for one, dx, dy in copies:
            pl.when(exists(-dx, -dy))(one.wait_recv)

    def gather(tile, at):
        cells = cell[tile, :, at]
        low, high = cells & (LANES - 1), cells >> 7
        line = lax.broadcasted_iota(jnp.int32, (chunks, LANES), 0)
        picked = jnp.take_along_axis(
            por[tile], jnp.broadcast_to(low, (chunks, LANES)), axis=1, mode="promise_in_bounds"
        )
        where_p[tile, :, at] = jnp.sum(jnp.where(line == high, picked, 0.0), axis=0, keepdims=True)
        low = jnp.broadcast_to(low, (8, LANES))
        high = jnp.broadcast_to(high, (8, LANES))
        found = [jnp.zeros((8, LANES), jnp.float32)] * (members // 8)
        for chunk in range(chunks):
            here = high == chunk
            for g in range(members // 8):
                part = sat[tile, 8 * g : 8 * (g + 1), chunk * LANES : (chunk + 1) * LANES]
                got = jnp.take_along_axis(part, low, axis=1, mode="promise_in_bounds")
                found[g] = jnp.where(here, got, found[g])
        for g in range(members // 8):
            seen[tile, 8 * g : 8 * (g + 1), at] = found[g]

    half = members // 2
    short = half + 8
    small_row = lax.broadcasted_iota(jnp.int32, (half, half), 0)
    small_lane = lax.broadcasted_iota(jnp.int32, (half, half), 1)
    lower, equal = small_row >= small_lane, small_row == small_lane
    spans = (slice(0, short), slice(short, short + members))

    def full(packed, tile):
        piece = packed[:half, tile * members : (tile + 1) * members]
        turned = jnp.transpose(piece)
        mixed, across = piece[:, :half], piece[:, half:]
        edge = packed[half : half + 1, tile * members : tile * members + half]
        top = jnp.where(lower, mixed, turned[:half])
        bottom = jnp.where(equal, edge, jnp.where(lower, turned[:half], mixed))
        return jnp.concatenate(
            [jnp.concatenate([top, across], axis=1), jnp.concatenate([turned[half:], bottom], axis=1)], axis=0
        )

    def statistics(step):
        def observe(block, carry):
            at = pl.ds(pl.multiple_of(block * LANES, LANES), LANES)
            for tile in range(tiles):
                pred[tile, :, at] = network(
                    seen[tile, :, at], where_p[tile, :, at], w_ref, b_ref, v_ref, c_ref
                )
            return carry

        lax.fori_loop(0, slots // LANES, observe, 0)
        found = [
            products(pred[tile], obs[tile], var[tile], count_ref[tile], pert[step, tile].astype(jnp.float32))
            for tile in range(tiles)
        ]
        own[step, short:] = jnp.concatenate([one[members:] for one in found], axis=1)
        own[step, :half] = jnp.concatenate(
            [
                piece
                for one in found
                for piece in (jnp.where(lower, one[:half, :half], one[half:members, half:]), one[:half, half:])
            ],
            axis=1,
        )
        edges = []
        for one in found:
            edge = jnp.sum(jnp.where(equal, one[half:members, half:], 0.0), axis=0, keepdims=True)
            edges += [edge, jnp.zeros_like(edge)]
        own[step, half:short] = jnp.broadcast_to(jnp.concatenate(edges, axis=1), (short - half, LANES))

    def weigh(s, cells, offset, count):
        departures = s - jnp.mean(s, axis=0, keepdims=True)
        x_row, x_column = centred(cells >> 6), centred(cells & (SIDE - 1))
        return [
            (departures * (hat(x_row, offset + a) * hat(x_column, b - 1.0))).astype(jnp.bfloat16)
            for a in range(count)
            for b in range(3)
        ]

    part = tile_cells // 2

    def place(half):
        cells = lax.broadcasted_iota(jnp.int32, (1, part), 1) + half * part
        return centred(cells >> 6), centred(cells & (SIDE - 1))

    def prepare(tile):
        for half in range(2):
            x_row, x_column = place(half)
            at = slice(half * part, (half + 1) * part)
            s = sat[tile, :, at]
            departures = s - jnp.mean(s, axis=0, keepdims=True)
            beside = jnp.where(x_column < 0.0, hat(x_column, -1.0), hat(x_column, 1.0))
            for q in range(4):
                factor = hat(x_row, half - 1.0 + q // 2) * (beside if q % 2 else hat(x_column, 0.0))
                ready[tile, q * members : (q + 1) * members, at] = (departures * factor).astype(jnp.bfloat16)

    def arrange(step, tile):
        for half in range(2):
            for b in range(2):
                for q in range(2):
                    row = b * members + q * (members // 2)
                    blend[tile, half, row : row + members // 2] = jnp.concatenate(
                        [
                            near[step, (1, 2 * b)[beside], tile + half + a][:, q * members : (q + 1) * members]
                            for a in range(2)
                            for beside in range(2)
                        ],
                        axis=1,
                    )

    def apply(tile, into):
        for half in range(2):
            at = slice(half * part, (half + 1) * part)
            moved = jnp.dot(blend[tile, half], ready[tile, :, at], preferred_element_type=jnp.float32)
            left = jnp.broadcast_to(place(half)[1] < 0.0, (members, part))
            into[tile, :, at] = sat[tile, :, at] + jnp.where(left, moved[:members], moved[members:])

    for load in loads[:-tiles]:
        load.wait()
    for tile in range(tiles):
        loads[tile - tiles].wait()

        def body(block, carry, tile=tile):
            gather(tile, pl.ds(pl.multiple_of(block * LANES, LANES), LANES))
            return carry

        lax.fori_loop(0, slots // LANES, body, 0)
    statistics(0)

    widen = (members - 1) * float(STEPS)
    unit = jnp.where(
        lax.broadcasted_iota(jnp.int32, (members, members), 0)
        == lax.broadcasted_iota(jnp.int32, (members, members), 1),
        1.0,
        0.0,
    )

    def swap(x):
        return jnp.concatenate([x[:, members:], x[:, :members]], axis=1)

    def sum_rows(step, at):
        mine, below, above = own[step, at], up_down[step, 0, at], up_down[step, 1, at]
        first = lax.broadcasted_iota(jnp.int32, mine.shape, 1) < members
        beside = W1 * (swap(mine) + jnp.where(first, swap(above), swap(below)))
        return mine + W2 * (above + below) + beside

    def sum_columns(step, at):
        near_by, far = side[step, 2, at] + side[step, 3, at], side[step, 0, at] + side[step, 1, at]
        return summed[step, at] + W1 * near_by + W2 * far

    pl.semaphore_wait(barrier, sum(jnp.where(exists(dx, dy), 1, 0) for dx, dy in partners))

    for step in range(STEPS):
        last = step + 1 == STEPS
        by_row = [
            start(
                step,
                2 * kind,
                [(own.at[step, at], up_down.at[step, i, at], dx, dy) for i, (dx, dy) in enumerate(rows)],
            )
            for kind, at in enumerate(spans)
        ]
        if last:
            for tile in range(tiles):
                arrange(step - 1, tile)
                apply(tile, sat)
        else:
            for tile in range(tiles):
                pieces = weigh(seen[tile], cell[tile], -1.0, 3)
                for q, piece in enumerate(pieces):
                    ready_seen[tile, q * members : (q + 1) * members] = piece
        by_column = []
        for kind, at in enumerate(spans):
            receive(by_row[kind])
            summed[step, at] = sum_rows(step, at)
            by_column.append(
                start(
                    step,
                    4 + 4 * kind,
                    [
                        (summed.at[step, at], side.at[step, i, at], dx, dy)
                        for i, (dx, dy) in enumerate(columns)
                    ],
                )
            )
        for tile in range(tiles):
            prepare(tile)
        receive(by_column[0])
        packed = sum_columns(step, spans[0])
        inverses = eliminate(
            [jnp.concatenate([full(packed, tile) + widen * unit, unit], axis=1) for tile in range(tiles)]
        )
        receive(by_column[1])
        pair = sum_columns(step, spans[1])
        for tile in range(tiles):
            turned = jnp.dot(
                pair[:, tile * members : (tile + 1) * members],
                inverses[tile][:, members:],
                precision=HIGHEST,
                preferred_element_type=jnp.float32,
            )
            near[step, 1, 1 + tile] = jnp.concatenate([turned[:half], turned[half:]], axis=1).astype(
                jnp.bfloat16
            )
        moves = []
        for dx, dy in around:
            if dx == 1:
                src, dst = near.at[step, 1, 2], near.at[step, 1 - dy, 0]
            elif dx == -1:
                src, dst = near.at[step, 1, 1], near.at[step, 1 - dy, 3]
            else:
                src, dst = near.at[step, 1, 1:3], near.at[step, 1 - dy, 1:3]
            moves.append((src, dst, dx, dy))
        receive(start(step, 12, moves))

        @pl.when(gx == 0)
        def _():
            near[step, :, 0] = near[step, :, 1]

        @pl.when(gx == nx - 1)
        def _():
            near[step, :, 3] = near[step, :, 2]

        @pl.when(gy == 0)
        def _():
            near[step, 0] = near[step, 1]

        @pl.when(gy == ny - 1)
        def _():
            near[step, 2] = near[step, 1]

        if not last:
            for tile in range(tiles):
                packed = [near[step, b, tile + a] for a in range(3) for b in range(3)]
                matrix = jnp.concatenate(
                    [
                        jnp.concatenate([one[:, q * members : (q + 1) * members] for one in packed], axis=1)
                        for q in range(2)
                    ],
                    axis=0,
                )
                moved = jnp.dot(matrix, ready_seen[tile], preferred_element_type=jnp.float32)
                seen[tile] = seen[tile] + moved
        if not last:
            statistics(step + 1)

    for tile in range(tiles):
        arrange(STEPS - 1, tile)
        apply(tile, out_ref)
    for one, dx, dy in late:
        pl.when(exists(dx, dy))(one.wait_send)


def per_device(
    saturation, porosity, observed_cells, observed_values, error_variance, observed_count, perturbation,
    input_weight, input_bias, output_weight, output_bias,
):
    row_tiles, column_tiles, members, tile_cells = saturation.shape
    slots = observed_cells.shape[2]
    tiles = row_tiles * column_tiles
    arrays = (
        saturation.reshape(tiles, members, tile_cells),
        porosity.reshape(tiles, tile_cells // LANES, LANES),
        observed_cells.reshape(tiles, 1, slots),
        observed_values.reshape(tiles, 1, slots),
        error_variance.reshape(tiles, 1, slots),
        perturbation.reshape(STEPS, tiles, members, slots),
    )
    scalars = (observed_count.reshape(tiles), input_weight, input_bias, output_weight, output_bias)
    f32, bf16 = jnp.float32, jnp.bfloat16
    lines = members // 2 + 8 + members
    posterior = pl.pallas_call(
        whole_kernel,
        name="assimilate",
        out_shape=jax.ShapeDtypeStruct((tiles, members, tile_cells), f32),
        in_specs=[pl.BlockSpec(memory_space=pltpu.HBM)] * (len(scalars) + len(arrays)),
        out_specs=pl.BlockSpec(memory_space=pltpu.VMEM),
        scratch_shapes=[pltpu.SMEM(a.shape, a.dtype) for a in scalars]
        + [pltpu.VMEM(a.shape, a.dtype) for a in arrays]
        + [
            pltpu.SemaphoreType.DMA((len(scalars) + len(arrays) - 1 + tiles,)),
            pltpu.VMEM((STEPS, lines, LANES), f32),
            pltpu.VMEM((STEPS, 2, lines, LANES), f32),
            pltpu.VMEM((STEPS, lines, LANES), f32),
            pltpu.VMEM((STEPS, 4, lines, LANES), f32),
            pltpu.VMEM((STEPS, 3, tiles + 2, members // 2, LANES), bf16),
            pltpu.VMEM((tiles, members, slots), f32),
            pltpu.VMEM((tiles, 1, slots), f32),
            pltpu.VMEM((tiles, members, slots), f32),
            pltpu.VMEM((tiles, 4 * members, tile_cells), bf16),
            pltpu.VMEM((tiles, 9 * members, slots), bf16),
            pltpu.VMEM((tiles, 2, 2 * members, 4 * members), bf16),
            pltpu.SemaphoreType.DMA((STEPS, 20)),
            pltpu.SemaphoreType.DMA((STEPS, 20)),
        ],
        compiler_params=pltpu.CompilerParams(
            collective_id=0, has_side_effects=True, vmem_limit_bytes=VMEM_LIMIT
        ),
    )(*(one if one.size == 1 else pltpu.with_memory_space_constraint(one, pltpu.HBM) for one in scalars + arrays))
    return posterior.reshape(row_tiles, column_tiles, members, tile_cells)


def solution(mesh):
    tile = P("gx", "gy", None)
    return jax.shard_map(
        per_device,
        mesh=mesh,
        in_specs=(
            P("gx", "gy", None, None), tile, tile, tile, tile, P("gx", "gy"),
            P(None, "gx", "gy", None, None), P(), P(), P(), P(),
        ),
        out_specs=P("gx", "gy", None, None),
        check_vma=False,
    )
```

```python
import math

import jax
import jax.numpy as jnp
from jax import lax
from jax.experimental import pallas as pl
from jax.experimental.pallas import tpu as pltpu
from jax.sharding import PartitionSpec as P

SIDE = 64
REACH = 2
STEPS = 2
LANES = 128
VMEM_LIMIT = 24 << 20
MESH = pl.DeviceIdType.MESH
HIGHEST = lax.Precision.HIGHEST
W1 = math.exp(-1.0 / (2.0 * REACH * REACH))
W2 = math.exp(-4.0 / (2.0 * REACH * REACH))


def network(s, p, w_ref, b_ref, v_ref, c_ref):
    total = jnp.zeros_like(s)
    for h in range(b_ref.shape[0]):
        inner = w_ref[0, h] * s + (w_ref[1, h] * p + b_ref[h])
        total = total + v_ref[h] * jnp.tanh(inner)
    return total + c_ref[0]


def products(predicted, observed, variance, count, shocks):
    slots = observed.shape[1]
    anomalies = predicted - jnp.mean(predicted, axis=0, keepdims=True)
    innovations = observed + jnp.sqrt(float(STEPS) * variance) * shocks - predicted
    active = lax.broadcasted_iota(jnp.int32, (1, slots), 1) < count
    scaled = anomalies * (jnp.where(active, 1.0, 0.0) / variance)
    both = jnp.concatenate([anomalies, innovations], axis=0)
    return lax.dot_general(
        both, scaled, (((1,), (1,)), ((), ())), precision=HIGHEST, preferred_element_type=jnp.float32
    )


def hat(x, offset):
    return jnp.maximum(0.0, 1.0 - jnp.abs(x - offset))


def centred(index):
    return (index.astype(jnp.float32) + 0.5) / SIDE - 0.5


def eliminate(matrices):
    group, width = 8, matrices[0].shape[1]
    groups = matrices[0].shape[0] // group
    row = lax.broadcasted_iota(jnp.int32, (group, width), 0)
    parts = [[m[group * h : group * (h + 1)] for h in range(groups)] for m in matrices]
    for g in range(groups):
        done = []
        for m in parts:
            pivots = [
                jnp.broadcast_to(m[g][:, group * g + i : group * g + i + 1], (group, width))
                for i in range(group)
            ]
            fresh = m[g]
            for j in range(group):
                inverse = 1.0 / pivots[j][j : j + 1]
                factor = jnp.where(row == j, -1.0, pivots[j])
                fresh = jnp.where(row == j, 0.0, fresh) - factor * (fresh[j : j + 1] * inverse)
                for i in range(j + 1, group):
                    pivots[i] = jnp.where(row == j, 0.0, pivots[i]) - factor * (pivots[i][j : j + 1] * inverse)
            new = []
            for h in range(groups):
                if h == g:
                    new.append(fresh)
                    continue
                taken = m[h][:, group * g : group * g + 1] * fresh[0:1]
                for i in range(1, group):
                    taken = taken + m[h][:, group * g + i : group * g + i + 1] * fresh[i : i + 1]
                new.append(m[h] - taken)
            done.append(new)
        parts = done
    return [jnp.concatenate(m, axis=0) for m in parts]


def whole_kernel(
    count_hbm, w_hbm, b_hbm, v_hbm, c_hbm,
    sat_hbm, por_hbm, cell_hbm, obs_hbm, var_hbm, pert_hbm,
    out_ref,
    count_ref, w_ref, b_ref, v_ref, c_ref,
    sat, por, cell, obs, var, pert, load_sem,
    own, up_down, summed, side, near, seen, where_p, pred, ready, ready_seen, blend,
    send_sem, recv_sem,
):
    nx, ny = lax.axis_size("gx"), lax.axis_size("gy")
    gx, gy = lax.axis_index("gx"), lax.axis_index("gy")
    tiles, members, tile_cells = sat.shape
    slots = seen.shape[2]
    chunks = tile_cells // LANES

    small = [(count_hbm, count_ref), (w_hbm, w_ref), (b_hbm, b_ref), (v_hbm, v_ref), (c_hbm, c_ref)]
    small += [(por_hbm, por), (cell_hbm, cell), (obs_hbm, obs), (var_hbm, var), (pert_hbm, pert)]
    loads = [pltpu.make_async_copy(src, dst, load_sem.at[i]) for i, (src, dst) in enumerate(small)]
    loads += [
        pltpu.make_async_copy(sat_hbm.at[t], sat.at[t], load_sem.at[len(small) + t]) for t in range(tiles)
    ]
    for load in loads:
        load.start()

    up_down[...] = jnp.zeros_like(up_down)
    side[...] = jnp.zeros_like(side)
    near[...] = jnp.zeros_like(near)

    def exists(dx, dy):
        there = True
        if dx:
            there = jnp.logical_and(gx + dx >= 0, gx + dx < nx)
        if dy:
            along = jnp.logical_and(gy + dy >= 0, gy + dy < ny)
            there = along if there is True else jnp.logical_and(there, along)
        return there

    def device(dx, dy):
        return (jnp.clip(gx + dx, 0, nx - 1), jnp.clip(gy + dy, 0, ny - 1))

    rows = [(-1, 0), (1, 0)]
    columns = [(0, -2), (0, 2), (0, -1), (0, 1)]
    around = [(dx, dy) for dx in (-1, 1, 0) for dy in (-1, 1, 0) if dx or dy]

    barrier = pltpu.get_barrier_semaphore()
    partners = sorted(set(rows + columns + around))
    for dx, dy in partners:

        @pl.when(exists(dx, dy))
        def _(dx=dx, dy=dy):
            pl.semaphore_signal(barrier, inc=1, device_id=device(dx, dy), device_id_type=MESH)

    late = []

    def start(step, first, moves):
        copies = []
        for i, (src, dst, dx, dy) in enumerate(moves):
            one = pltpu.make_async_remote_copy(
                src_ref=src,
                dst_ref=dst,
                send_sem=send_sem.at[step, first + i],
                recv_sem=recv_sem.at[step, first + i],
                device_id=device(dx, dy),
                device_id_type=MESH,
            )
            pl.when(exists(dx, dy))(one.start)
            copies.append((one, dx, dy))
        late.extend(copies)
        return copies

    def receive(copies):
        for one, dx, dy in copies:
            pl.when(exists(-dx, -dy))(one.wait_recv)

    def gather(tile, at):
        cells = cell[tile, :, at]
        low, high = cells & (LANES - 1), cells >> 7
        line = lax.broadcasted_iota(jnp.int32, (chunks, LANES), 0)
        picked = jnp.take_along_axis(
            por[tile], jnp.broadcast_to(low, (chunks, LANES)), axis=1, mode="promise_in_bounds"
        )
        where_p[tile, :, at] = jnp.sum(jnp.where(line == high, picked, 0.0), axis=0, keepdims=True)
        low = jnp.broadcast_to(low, (8, LANES))
        high = jnp.broadcast_to(high, (8, LANES))
        found = [jnp.zeros((8, LANES), jnp.float32)] * (members // 8)
        for chunk in range(chunks):
            here = high == chunk
            for g in range(members // 8):
                part = sat[tile, 8 * g : 8 * (g + 1), chunk * LANES : (chunk + 1) * LANES]
                got = jnp.take_along_axis(part, low, axis=1, mode="promise_in_bounds")
                found[g] = jnp.where(here, got, found[g])
        for g in range(members // 8):
            seen[tile, 8 * g : 8 * (g + 1), at] = found[g]

    half = members // 2
    short = half + 8
    small_row = lax.broadcasted_iota(jnp.int32, (half, half), 0)
    small_lane = lax.broadcasted_iota(jnp.int32, (half, half), 1)
    lower, equal = small_row >= small_lane, small_row == small_lane
    spans = (slice(0, short), slice(short, short + members))

    def full(packed, tile):
        piece = packed[:half, tile * members : (tile + 1) * members]
        turned = jnp.transpose(piece)
        mixed, across = piece[:, :half], piece[:, half:]
        edge = packed[half : half + 1, tile * members : tile * members + half]
        top = jnp.where(lower, mixed, turned[:half])
        bottom = jnp.where(equal, edge, jnp.where(lower, turned[:half], mixed))
        return jnp.concatenate(
            [jnp.concatenate([top, across], axis=1), jnp.concatenate([turned[half:], bottom], axis=1)], axis=0
        )

    def predict(tile, at):
        pred[tile, :, at] = network(seen[tile, :, at], where_p[tile, :, at], w_ref, b_ref, v_ref, c_ref)

    def statistics(step):
        def observe(block, carry):
            at = pl.ds(pl.multiple_of(block * LANES, LANES), LANES)
            for tile in range(0 if step else tiles - 1, tiles):
                predict(tile, at)
            return carry

        lax.fori_loop(0, slots // LANES, observe, 0)
        found = [
            products(pred[tile], obs[tile], var[tile], count_ref[tile], pert[step, tile].astype(jnp.float32))
            for tile in range(tiles)
        ]
        own[step, short:] = jnp.concatenate([one[members:] for one in found], axis=1)
        own[step, :half] = jnp.concatenate(
            [
                piece
                for one in found
                for piece in (jnp.where(lower, one[:half, :half], one[half:members, half:]), one[:half, half:])
            ],
            axis=1,
        )
        edges = []
        for one in found:
            edge = jnp.sum(jnp.where(equal, one[half:members, half:], 0.0), axis=0, keepdims=True)
            edges += [edge, jnp.zeros_like(edge)]
        own[step, half:short] = jnp.broadcast_to(jnp.concatenate(edges, axis=1), (short - half, LANES))

    def weigh(s, cells, offset, count):
        departures = s - jnp.mean(s, axis=0, keepdims=True)
        x_row, x_column = centred(cells >> 6), centred(cells & (SIDE - 1))
        return [
            (departures * (hat(x_row, offset + a) * hat(x_column, b - 1.0))).astype(jnp.bfloat16)
            for a in range(count)
            for b in range(3)
        ]

    part = tile_cells // 2

    def place(half):
        cells = lax.broadcasted_iota(jnp.int32, (1, part), 1) + half * part
        return centred(cells >> 6), centred(cells & (SIDE - 1))

    def prepare(tile):
        for half in range(2):
            x_row, x_column = place(half)
            at = slice(half * part, (half + 1) * part)
            s = sat[tile, :, at]
            departures = s - jnp.mean(s, axis=0, keepdims=True)
            beside = jnp.where(x_column < 0.0, hat(x_column, -1.0), hat(x_column, 1.0))
            for q in range(4):
                factor = hat(x_row, half - 1.0 + q // 2) * (beside if q % 2 else hat(x_column, 0.0))
                ready[tile, q * members : (q + 1) * members, at] = (departures * factor).astype(jnp.bfloat16)

    def arrange(step, tile):
        for half in range(2):
            for b in range(2):
                for q in range(2):
                    row = b * members + q * (members // 2)
                    blend[tile, half, row : row + members // 2] = jnp.concatenate(
                        [
                            near[step, (1, 2 * b)[beside], tile + half + a][:, q * members : (q + 1) * members]
                            for a in range(2)
                            for beside in range(2)
                        ],
                        axis=1,
                    )

    def apply(tile, into):
        for half in range(2):
            at = slice(half * part, (half + 1) * part)
            moved = jnp.dot(blend[tile, half], ready[tile, :, at], preferred_element_type=jnp.float32)
            left = jnp.broadcast_to(place(half)[1] < 0.0, (members, part))
            into[tile, :, at] = sat[tile, :, at] + jnp.where(left, moved[:members], moved[members:])

    for load in loads[:-tiles]:
        load.wait()
    for tile in range(tiles):
        loads[tile - tiles].wait()

        def body(block, carry, tile=tile):
            at = pl.ds(pl.multiple_of(block * LANES, LANES), LANES)
            gather(tile, at)
            if tile:
                predict(tile - 1, at)
            return carry

        lax.fori_loop(0, slots // LANES, body, 0)
    statistics(0)

    widen = (members - 1) * float(STEPS)
    unit = jnp.where(
        lax.broadcasted_iota(jnp.int32, (members, members), 0)
        == lax.broadcasted_iota(jnp.int32, (members, members), 1),
        1.0,
        0.0,
    )

    def swap(x):
        return jnp.concatenate([x[:, members:], x[:, :members]], axis=1)

    def sum_rows(step, at):
        mine, below, above = own[step, at], up_down[step, 0, at], up_down[step, 1, at]
        first = lax.broadcasted_iota(jnp.int32, mine.shape, 1) < members
        beside = W1 * (swap(mine) + jnp.where(first, swap(above), swap(below)))
        return mine + W2 * (above + below) + beside

    def sum_columns(step, at):
        near_by, far = side[step, 2, at] + side[step, 3, at], side[step, 0, at] + side[step, 1, at]
        return summed[step, at] + W1 * near_by + W2 * far

    pl.semaphore_wait(barrier, sum(jnp.where(exists(dx, dy), 1, 0) for dx, dy in partners))

    for step in range(STEPS):
        last = step + 1 == STEPS
        by_row = [
            start(
                step,
                2 * kind,
                [(own.at[step, at], up_down.at[step, i, at], dx, dy) for i, (dx, dy) in enumerate(rows)],
            )
            for kind, at in enumerate(spans)
        ]
        if last:
            for tile in range(tiles):
                arrange(step - 1, tile)
                apply(tile, sat)
        else:
            for tile in range(tiles):
                pieces = weigh(seen[tile], cell[tile], -1.0, 3)
                for q, piece in enumerate(pieces):
                    ready_seen[tile, q * members : (q + 1) * members] = piece
        by_column = []
        for kind, at in enumerate(spans):
            receive(by_row[kind])
            summed[step, at] = sum_rows(step, at)
            by_column.append(
                start(
                    step,
                    4 + 4 * kind,
                    [
                        (summed.at[step, at], side.at[step, i, at], dx, dy)
                        for i, (dx, dy) in enumerate(columns)
                    ],
                )
            )
        for tile in range(tiles):
            prepare(tile)
        receive(by_column[0])
        packed = sum_columns(step, spans[0])
        inverses = eliminate(
            [jnp.concatenate([full(packed, tile) + widen * unit, unit], axis=1) for tile in range(tiles)]
        )
        receive(by_column[1])
        pair = sum_columns(step, spans[1])
        for tile in range(tiles):
            turned = jnp.dot(
                pair[:, tile * members : (tile + 1) * members],
                inverses[tile][:, members:],
                precision=HIGHEST,
                preferred_element_type=jnp.float32,
            )
            near[step, 1, 1 + tile] = jnp.concatenate([turned[:half], turned[half:]], axis=1).astype(
                jnp.bfloat16
            )
        moves = []
        for dx, dy in around:
            if dx == 1:
                src, dst = near.at[step, 1, 2], near.at[step, 1 - dy, 0]
            elif dx == -1:
                src, dst = near.at[step, 1, 1], near.at[step, 1 - dy, 3]
            else:
                src, dst = near.at[step, 1, 1:3], near.at[step, 1 - dy, 1:3]
            moves.append((src, dst, dx, dy))
        receive(start(step, 12, moves))

        @pl.when(gx == 0)
        def _():
            near[step, :, 0] = near[step, :, 1]

        @pl.when(gx == nx - 1)
        def _():
            near[step, :, 3] = near[step, :, 2]

        @pl.when(gy == 0)
        def _():
            near[step, 0] = near[step, 1]

        @pl.when(gy == ny - 1)
        def _():
            near[step, 2] = near[step, 1]

        if not last:
            for tile in range(tiles):
                packed = [near[step, b, tile + a] for a in range(3) for b in range(3)]
                matrix = jnp.concatenate(
                    [
                        jnp.concatenate([one[:, q * members : (q + 1) * members] for one in packed], axis=1)
                        for q in range(2)
                    ],
                    axis=0,
                )
                moved = jnp.dot(matrix, ready_seen[tile], preferred_element_type=jnp.float32)
                seen[tile] = seen[tile] + moved
        if not last:
            statistics(step + 1)

    for tile in range(tiles):
        arrange(STEPS - 1, tile)
        apply(tile, out_ref)
    for one, dx, dy in late:
        pl.when(exists(dx, dy))(one.wait_send)


def per_device(
    saturation, porosity, observed_cells, observed_values, error_variance, observed_count, perturbation,
    input_weight, input_bias, output_weight, output_bias,
):
    row_tiles, column_tiles, members, tile_cells = saturation.shape
    slots = observed_cells.shape[2]
    tiles = row_tiles * column_tiles
    arrays = (
        saturation.reshape(tiles, members, tile_cells),
        porosity.reshape(tiles, tile_cells // LANES, LANES),
        observed_cells.reshape(tiles, 1, slots),
        observed_values.reshape(tiles, 1, slots),
        error_variance.reshape(tiles, 1, slots),
        perturbation.reshape(STEPS, tiles, members, slots),
    )
    scalars = (observed_count.reshape(tiles), input_weight, input_bias, output_weight, output_bias)
    f32, bf16 = jnp.float32, jnp.bfloat16
    lines = members // 2 + 8 + members
    posterior = pl.pallas_call(
        whole_kernel,
        name="assimilate",
        out_shape=jax.ShapeDtypeStruct((tiles, members, tile_cells), f32),
        in_specs=[pl.BlockSpec(memory_space=pltpu.HBM)] * (len(scalars) + len(arrays)),
        out_specs=pl.BlockSpec(memory_space=pltpu.VMEM),
        scratch_shapes=[pltpu.SMEM(a.shape, a.dtype) for a in scalars]
        + [pltpu.VMEM(a.shape, a.dtype) for a in arrays]
        + [
            pltpu.SemaphoreType.DMA((len(scalars) + len(arrays) - 1 + tiles,)),
            pltpu.VMEM((STEPS, lines, LANES), f32),
            pltpu.VMEM((STEPS, 2, lines, LANES), f32),
            pltpu.VMEM((STEPS, lines, LANES), f32),
            pltpu.VMEM((STEPS, 4, lines, LANES), f32),
            pltpu.VMEM((STEPS, 3, tiles + 2, members // 2, LANES), bf16),
            pltpu.VMEM((tiles, members, slots), f32),
            pltpu.VMEM((tiles, 1, slots), f32),
            pltpu.VMEM((tiles, members, slots), f32),
            pltpu.VMEM((tiles, 4 * members, tile_cells), bf16),
            pltpu.VMEM((tiles, 9 * members, slots), bf16),
            pltpu.VMEM((tiles, 2, 2 * members, 4 * members), bf16),
            pltpu.SemaphoreType.DMA((STEPS, 20)),
            pltpu.SemaphoreType.DMA((STEPS, 20)),
        ],
        compiler_params=pltpu.CompilerParams(
            collective_id=0, has_side_effects=True, vmem_limit_bytes=VMEM_LIMIT
        ),
    )(*(one if one.size == 1 else pltpu.with_memory_space_constraint(one, pltpu.HBM) for one in scalars + arrays))
    return posterior.reshape(row_tiles, column_tiles, members, tile_cells)


def solution(mesh):
    tile = P("gx", "gy", None)
    return jax.shard_map(
        per_device,
        mesh=mesh,
        in_specs=(
            P("gx", "gy", None, None), tile, tile, tile, tile, P("gx", "gy"),
            P(None, "gx", "gy", None, None), P(), P(), P(), P(),
        ),
        out_specs=P("gx", "gy", None, None),
        check_vma=False,
    )
```
